256 devices in a mesh: row: 16 (over z_hi, x), col: 16 (over y, z_lo, core).
Axes of the slice: x: 4, y: 4, z: 8 (z_hi: 4, z_lo: 2; z = z_hi * 2 + z_lo), core: 2. Of those that a mesh axis runs over, the one named last changes fastest.
Arguments:
- panels: int32 [1], replicated, may hold values from 0 to 15
- inverse: float32 [16384, 16384], P('row', 'col'), may hold values from -4 to 28, as said below
- weight: float32 [1024, 16384], P('row', 'col'), may hold values from -0.046875 to 0.046875
- tokens: bfloat16 [2048, 16384], P('row', 'col'), may hold values from -6 to 6
- targets: bfloat16 [2048, 1024], P('row', 'col'), may hold values from -6 to 6
Outputs:
- new_inverse: float32 [16384, 16384], P('row', 'col')
- pruned: float32 [1024, 16384], P('row', 'col')
- residual: float32 [2048, 1024], P('row', 'col')
- correlation: float32 [1024, 16384], P('row', 'col')
The draws below stay inside these ranges and needn't reach their ends.
Inputs may be any that keep to these rules, and one draw needn't show every extreme that they name: `inverse`: symmetric and positive definite.
All inputs are finite; a program needn't handle non-finite values.
Results may differ from the reference program's by a relative error of at most 0.0035.
Values may be sent and summed in bfloat16 or wider, within the bound.
A program may use at most 128 MiB of HBM per device.

```python
import math
import jax
import jax.numpy as jnp
from jax import lax

D = 16384
PW = 1024
OUT = 1024
ROUNDS = 1
TOKENS = 2048


def draw_inverse(key, part):
    key_noise = jax.random.fold_in(key, 11)
    key_diag = jax.random.fold_in(key, 12)
    key_coupling = jax.random.fold_in(key, 14)
    key_signs = jax.random.fold_in(key, 15)
    gaussian = jnp.clip(jax.random.normal(key_noise, (D, D), jnp.float32), -6.0, 6.0)
    symmetric = (gaussian + gaussian.T) * (0.5 / math.sqrt(2.0 * D))
    diagonal = jax.random.uniform(key_diag, (D,), jnp.float32, 1.5, 3.0)
    coupling = jnp.exp(jax.random.uniform(key_coupling, (D,), jnp.float32, math.log(0.5), math.log(2.0)))
    reach_length = max(PW / 32.0, 2.0)
    position = jnp.arange(D, dtype=jnp.float32)
    distance = jnp.abs(position[:, None] - position[None, :])
    kernel = 0.25 * jnp.exp(-distance / reach_length) * coupling[:, None] * coupling[None, :]
    inner_width = D // 16
    signs = jnp.where(jax.random.bernoulli(key_signs, 0.5, (D, inner_width)), 1.0, -1.0).astype(jnp.float32)
    gram = jnp.dot(signs, signs.T, precision=lax.Precision.HIGHEST, preferred_element_type=jnp.float32) * (1.0 / inner_width)
    matrix = kernel + symmetric + gram + jnp.diag(diagonal)
    return matrix.astype(jnp.float32)


def steps_of(own_key, dims, cuts, smallest, top_value):
    gain, own = 1.0, jax.random.fold_in(own_key, 6)
    for dim, blocks in cuts:
        heights = jnp.exp(jax.random.uniform(jax.random.fold_in(own, dim), (blocks,), jnp.float32, smallest / len(cuts), top_value / len(cuts)))
        gain = gain * jnp.repeat(heights, dims[dim] // blocks).reshape([-1 if axis == dim else 1 for axis in range(len(dims))])
    return gain


def centred(rng, dims, width, reach, split=(), held_as=jnp.bfloat16):
    array = jax.random.normal(rng, dims, jnp.float32) * width
    if len(split) > 0:
        array = steps_of(rng, dims, split, -0.22, 0.18) * array
    return jnp.clip(array, min=-reach, max=reach).astype(held_as)


def setup_inputs(seed: int = 0) -> dict:
    key_list = jax.random.split(jax.random.key(seed), 6)
    panels = jax.random.randint(key_list[0], (ROUNDS,), 0, D // PW).astype(jnp.int32)
    inverse = draw_inverse(jax.random.fold_in(key_list[5], 71), 0)
    weight = centred(key_list[2], (OUT, D), D ** -0.5, 0.046875, ((0, 16), (1, 16)), jnp.float32)
    tokens = centred(key_list[3], (TOKENS, D), 1.0, 6.0, ((0, 16), (1, 16)))
    targets = centred(key_list[4], (TOKENS, OUT), 1.0, 6.0, ((0, 16), (1, 16)))
    return {"panels": panels, "inverse": inverse, "weight": weight, "tokens": tokens, "targets": targets}


def reference(panels, inverse, weight, tokens, targets):
    highest = lax.Precision.HIGHEST
    anchor = (panels[0] * PW).astype(jnp.int32)
    column = lax.dynamic_slice_in_dim(inverse, anchor, PW, 1)
    row_panel = lax.dynamic_slice_in_dim(inverse, anchor, PW, 0)
    diag_block = lax.dynamic_slice_in_dim(row_panel, anchor, PW, 1)
    factor = jnp.linalg.cholesky(diag_block)
    halfway = lax.linalg.triangular_solve(factor, row_panel, left_side=True, lower=True, transpose_a=False)
    solved = lax.linalg.triangular_solve(factor, halfway, left_side=True, lower=True, transpose_a=True)
    new_inverse = inverse - jnp.dot(column.astype(jnp.float32), solved.astype(jnp.float32), precision=highest, preferred_element_type=jnp.float32)
    weight_cols = lax.dynamic_slice_in_dim(weight, anchor, PW, 1)
    pruned = weight - jnp.dot(weight_cols.astype(jnp.float32), solved.astype(jnp.float32), precision=highest, preferred_element_type=jnp.float32)
    pruned_low = pruned.astype(jnp.bfloat16)
    residual = jnp.dot(tokens.astype(jnp.float32), pruned_low.T.astype(jnp.float32), preferred_element_type=jnp.float32) - targets.astype(jnp.float32)
    residual_low = residual.astype(jnp.bfloat16)
    correlation = jnp.dot(residual_low.T.astype(jnp.float32), tokens.astype(jnp.float32), preferred_element_type=jnp.float32) * (1.0 / math.sqrt(TOKENS))
    return (new_inverse, pruned, residual, correlation)
```

```python
import functools
import math

import jax
import jax.numpy as jnp
from jax import lax
from jax.experimental import pallas as pl
from jax.experimental.pallas import tpu as pltpu
from jax.sharding import PartitionSpec as P

PW = 1024
NB = 128
MESH = pl.DeviceIdType.MESH
VMEM = pl.BlockSpec(memory_space=pltpu.VMEM)
f32 = jnp.float32
bf16 = jnp.bfloat16


def place():
    i, j = lax.axis_index("row"), lax.axis_index("col")
    return i, j, i // 4, i % 4, j // 4, (j // 2) % 2, j % 2


def row_of(zh, x):
    return (zh % 4) * 4 + x % 4


def col_of(y, zl, c):
    return ((y % 4) * 2 + zl % 2) * 2 + c % 2


class Copies:
    def __init__(self, send, recv):
        self.send, self.recv, self.made = send, recv, []

    def __call__(self, src, dst, device):
        n = len(self.made)
        copy = pltpu.make_async_remote_copy(
            src_ref=src,
            dst_ref=dst,
            send_sem=self.send.at[n],
            recv_sem=self.recv.at[n],
            device_id=device,
            device_id_type=MESH,
        )
        copy.start()
        self.made.append(copy)
        return copy

    def drain(self):
        for copy in self.made:
            copy.wait_send()


def meet(devices):
    barrier = pltpu.get_barrier_semaphore()
    for device in devices:
        pl.semaphore_signal(barrier, inc=1, device_id=device, device_id_type=MESH)
    pl.semaphore_wait(barrier, len(devices))


PR, PC = 32, 1152


def block_kernel(p_ref, h_ref, out_ref, pack, chunk, got, mine, zgot, local, send1, recv1, send, recv):
    i, j, zh, x, y, zl, c = place()
    p = p_ref[0]
    xs = [(row_of(zh, x + d), j) for d in (1, 2, 3)]
    zs = [(row_of(zh + d, x), j) for d in (1, 2, 3)]
    meet([(i, (j + d) % 16) for d in range(1, 16)] + xs + zs)

    scatter = [
        pltpu.make_async_remote_copy(
            src_ref=pack.at[pl.ds(pl.multiple_of(((j + d) % 16) * PR, PR), PR)],
            dst_ref=chunk,
            send_sem=send1.at[d - 1],
            recv_sem=recv1,
            device_id=(i, (j + d) % 16),
            device_id_type=MESH,
        )
        for d in range(1, 16)
    ]

    @pl.when(i == j)
    def _():
        loads = []
        for g in range(4):
            rows = pl.ds(128 * g, 128)
            a, b = 128 * (g + 1), 128 * (8 - g)
            loads.append(pltpu.make_async_copy(h_ref.at[rows, pl.ds(0, a)], pack.at[rows, pl.ds(0, a)], local.at[2 * g]))
            far = pl.ds(128 * (7 - g), 128)
            loads.append(pltpu.make_async_copy(h_ref.at[far, pl.ds(0, b)], pack.at[rows, pl.ds(a, b)], local.at[2 * g + 1]))
        for load in loads:
            load.start()
        for load in loads:
            load.wait()
        for copy in scatter:
            copy.start()
        own = pltpu.make_async_copy(pack.at[pl.ds(pl.multiple_of(j * PR, PR), PR)], chunk, local.at[8])
        own.start()
        own.wait()

    @pl.when(i != j)
    def _():
        scatter[0].wait_recv()

    copies = Copies(send, recv)

    def piece(k):
        return pl.ds(pl.multiple_of((k % 4) * 8, 8), 8)

    firsts = [copies(chunk.at[piece(x + d)], got.at[d - 1], xs[d - 1]) for d in (1, 2, 3)]
    held = jnp.where(i == p, chunk[piece(x), :], 0.0)
    for d in (1, 2, 3):
        firsts[d - 1].wait_recv()
        held = held + jnp.where(row_of(zh, x - d + 4) == p, got[d - 1], 0.0)
    mine[...] = held
    seconds = [copies(mine, zgot.at[d - 1], zs[d - 1]) for d in (1, 2, 3)]
    for d in (1, 2, 3):
        seconds[d - 1].wait_recv()
        held = held + zgot[d - 1]
    out_ref[j, piece(x), :] = held
    thirds = [copies(out_ref.at[j, piece(x)], out_ref.at[j, piece(x)], xs[d - 1]) for d in (1, 2, 3)]
    for copy in thirds:
        copy.wait_recv()

    gather_cols(copies, out_ref, out_ref, PR)
    copies.drain()

    @pl.when(i == j)
    def _():
        for copy in scatter:
            copy.wait_send()


def gather_cols(copies, first, out, rows):
    i, j, zh, x, y, zl, c = place()
    h = rows // 2
    ups, downs, cores = [], [], []
    across = copies(first.at[j], out.at[j], (i, col_of(y, zl + 1, c)))
    up, down = (i, col_of(y + 1, zl, c)), (i, col_of(y + 3, zl, c))
    peer = (i, col_of(y, zl, c + 1))
    for t in (0, 1):
        src = first if t == 0 else out
        if t == 1:
            across.wait_recv()
        s = col_of(y, zl + t, c)
        ups.append(copies(src.at[s], out.at[s], up))
        downs.append(copies(src.at[s], out.at[s], down))
        cores.append(copies(src.at[s], out.at[s], peer))
    halves = []
    for t in (0, 1):
        ups[t].wait_recv()
        s = col_of(y + 3, zl + t, c)
        halves.append(copies(out.at[s, pl.ds(0, h)], out.at[s, pl.ds(0, h)], up))
        cores.append(copies(out.at[s], out.at[s], peer))
        downs[t].wait_recv()
        s = col_of(y + 1, zl + t, c)
        halves.append(copies(out.at[s, pl.ds(h, h)], out.at[s, pl.ds(h, h)], down))
        cores.append(copies(out.at[s], out.at[s], peer))
    for t in (0, 1):
        halves[2 * t].wait_recv()
        halves[2 * t + 1].wait_recv()
        s = col_of(y + 2, zl + t, c)
        cores.append(copies(out.at[s], out.at[s], peer))
    for copy in cores:
        copy.wait_recv()


def block_everywhere(panels, inverse):
    sems = 9 + 25
    return pl.pallas_call(
        block_kernel,
        out_shape=jax.ShapeDtypeStruct((16, PR, PC), f32),
        in_specs=[pl.BlockSpec(memory_space=pltpu.SMEM), pl.BlockSpec(memory_space=pl.ANY)],
        out_specs=VMEM,
        scratch_shapes=[
            pltpu.VMEM((16 * PR, PC), f32),
            pltpu.VMEM((PR, PC), f32),
            pltpu.VMEM((3, 8, PC), f32),
            pltpu.VMEM((8, PC), f32),
            pltpu.VMEM((3, 8, PC), f32),
            pltpu.SemaphoreType.DMA((9,)),
            pltpu.SemaphoreType.DMA((15,)),
            pltpu.SemaphoreType.DMA,
            pltpu.SemaphoreType.DMA((sems,)),
            pltpu.SemaphoreType.DMA((sems,)),
        ],
        compiler_params=pltpu.CompilerParams(collective_id=0, has_side_effects=True, vmem_limit_bytes=24 << 20),
        cost_estimate=pl.CostEstimate(flops=10**9, bytes_accessed=160 * 10**6, transcendentals=0),
        name="block_everywhere",
    )(panels, inverse)


def split(x):
    hi = x.astype(bf16)
    return hi, (x - hi.astype(f32)).astype(bf16)


def dot(a, b):
    return jnp.dot(a, b, preferred_element_type=f32)


def dot3(a, b):
    ah, al = split(a)
    bh, bl = split(b)
    return dot(ah, bh) + (dot(ah, bl) + dot(al, bh))


def pivot_inverse(rows):
    lane = lax.broadcasted_iota(jnp.int32, (8, NB), 1)
    sub = lax.broadcasted_iota(jnp.int32, (8, NB), 0)
    lane1 = lax.broadcasted_iota(jnp.int32, (1, NB), 1)
    rows = list(rows)
    for k in range(0, NB, 2):
        v, s = k // 8, k % 8
        c0 = [jnp.broadcast_to(r[:, k : k + 1], (8, NB)) for r in rows]
        c1 = [jnp.broadcast_to(r[:, k + 1 : k + 2], (8, NB)) for r in rows]
        r0, r1 = rows[v][s : s + 1, :], rows[v][s + 1 : s + 2, :]
        p00, p01 = c0[v][s : s + 1, :], c1[v][s : s + 1, :]
        p10, p11 = c0[v][s + 1 : s + 2, :], c1[v][s + 1 : s + 2, :]
        scale = 1.0 / (p00 * p11 - p01 * p10)
        e0, e1 = lane1 == k, lane1 == k + 1
        r0 = jnp.where(e0, 1.0, jnp.where(e1, 0.0, r0))
        r1 = jnp.where(e1, 1.0, jnp.where(e0, 0.0, r1))
        u0 = jnp.broadcast_to((p11 * scale) * r0 - (p01 * scale) * r1, (8, NB))
        u1 = jnp.broadcast_to((p00 * scale) * r1 - (p10 * scale) * r0, (8, NB))
        cols = (lane == k) | (lane == k + 1)
        for w in range(NB // 8):
            base = jnp.where(cols, 0.0, rows[w]) - c0[w] * u0 - c1[w] * u1
            if w == v:
                base = jnp.where(sub == s, u0, jnp.where(sub == s + 1, u1, base))
            rows[w] = base
    return rows


def inverse_kernel(b_ref, a, piv):
    n = PW
    for g in range(4):
        for r, start in ((g, 0), (7 - g, 128 * (g + 1))):
            for q in range(r + 1):
                lanes = pl.ds(start + 128 * q, 128)
                tile = jnp.concatenate([b_ref[4 * g + m, :, lanes] for m in range(4)], axis=0)
                a[pl.ds(128 * r, 128), pl.ds(128 * q, 128)] = tile
                if q < r:
                    a[pl.ds(128 * q, 128), pl.ds(128 * r, 128)] = tile.T
    eye = (lax.broadcasted_iota(jnp.int32, (NB, NB), 0) == lax.broadcasted_iota(jnp.int32, (NB, NB), 1)).astype(f32)

    def step(kb, _):
        at = pl.ds(pl.multiple_of(kb * NB, NB), NB)
        blk = [a[pl.ds(pl.multiple_of(kb * NB + 8 * w, 8), 8), at] for w in range(NB // 8)]
        inv = pivot_inverse(blk)
        for w in range(NB // 8):
            piv[8 * w : 8 * w + 8, :] = inv[w]
        a[at, at] = eye
        u = dot3(piv[...], a[at, :])
        uh, ul = split(u)
        a[at, at] = -eye
        ch, cl = split(a[:, at])
        a[at, :] = jnp.zeros((NB, n), f32)
        a[:, at] = jnp.zeros((n, NB), f32)
        uk = jnp.concatenate([uh, ul, uh], axis=0)
        ck = jnp.concatenate([ch, ch, cl], axis=1)
        for t in range(n // 256):
            r = slice(256 * t, 256 * t + 256)
            a[r, :] = a[r, :] - dot(ck[r, :], uk)
        return 0

    lax.fori_loop(0, n // NB, step, 0)


def panel_inverse(packed):
    return pl.pallas_call(
        inverse_kernel,
        out_shape=jax.ShapeDtypeStruct((PW, PW), f32),
        in_specs=[VMEM],
        out_specs=VMEM,
        scratch_shapes=[pltpu.VMEM((NB, NB), f32)],
        compiler_params=pltpu.CompilerParams(vmem_limit_bytes=40 << 20),
        cost_estimate=pl.CostEstimate(flops=60 * 10**9, bytes_accessed=200 * 10**6, transcendentals=0),
        name="panel_inverse",
    )(packed)


def refresh_kernel(
    scale, low_ref, tok_ref, tgt_ref, res_ref, cor_ref, every, part, heard, own_low, lows,
    s_far, r_far_up, r_far_down, s_up, s_down, r_up, r_down, own,
    z_far, zr_far_up, zr_far_down, z_up, z_down, zr_up, zr_down,
    send, recv, rs_send, rs_recv, ag_send, ag_recv,
):
    i, j, zh, x, y, zl, c = place()
    x_up, x_down = (row_of(zh, x + 1), j), (row_of(zh, x + 3), j)
    z_next, z_prev = (row_of(zh + 1, x), j), (row_of(zh + 3, x), j)
    meet([(i, (j + d) % 16) for d in range(1, 16)] + [x_up, x_down, z_next, z_prev])
    copies = Copies(send, recv)
    tokens = tok_ref[...]
    half = low_ref.shape[0] // 2
    top, bottom = pl.ds(0, half), pl.ds(half, half)

    partials = []

    def use(s, block):
        value = lax.dot_general(block[...], tokens, (((1,), (1,)), ((), ())), preferred_element_type=f32)
        part[s] = value
        copy = pltpu.make_async_remote_copy(
            src_ref=part.at[s],
            dst_ref=heard.at[j],
            send_sem=rs_send.at[s],
            recv_sem=rs_recv.at[j],
            device_id=(i, s),
            device_id_type=MESH,
        )
        pl.when(s != j)(copy.start)
        partials.append((s, copy))

    def spread(s, block):
        return s, copies(block, every.at[s], x_up), copies(block, every.at[s], x_down)

    zn = copies(low_ref, every.at[i], z_next)
    zp = copies(low_ref, every.at[i], z_prev)
    sent = [spread(i, low_ref)]
    use(i, low_ref)
    zn.wait_recv()
    s = row_of(zh + 3, x)
    z1 = copies(every.at[s, top], every.at[s, top], z_next)
    sent.append(spread(s, every.at[s]))
    zp.wait_recv()
    s = row_of(zh + 1, x)
    z2 = copies(every.at[s, bottom], every.at[s, bottom], z_prev)
    sent.append(spread(s, every.at[s]))
    use(row_of(zh + 3, x), every.at[row_of(zh + 3, x)])
    use(s, every.at[s])
    z1.wait_recv()
    z2.wait_recv()
    s = row_of(zh + 2, x)
    sent.append(spread(s, every.at[s]))
    use(s, every.at[s])
    lasts = []
    for dz, (_, up, down) in zip((0, 3, 1, 2), sent):
        up.wait_recv()
        s = row_of(zh + dz, x + 3)
        a = copies(every.at[s, top], every.at[s, top], x_up)
        use(s, every.at[s])
        down.wait_recv()
        s = row_of(zh + dz, x + 1)
        b = copies(every.at[s, bottom], every.at[s, bottom], x_down)
        use(s, every.at[s])
        lasts.append((dz, a, b))
    for dz, a, b in lasts:
        a.wait_recv()
        b.wait_recv()
        s = row_of(zh + dz, x + 2)
        use(s, every.at[s])

    total = part[j] - tgt_ref[...]
    for d in range(1, 16):
        k = (j + d) % 16
        pltpu.make_async_remote_copy(
            src_ref=part.at[k],
            dst_ref=heard.at[k],
            send_sem=rs_send.at[k],
            recv_sem=rs_recv.at[k],
            device_id=(i, k),
            device_id_type=MESH,
        ).wait_recv()
        total = total + heard[k]
    res_ref[...] = total
    own_low[...] = total.astype(bf16)

    shared = []
    for d in range(1, 16):
        copy = pltpu.make_async_remote_copy(
            src_ref=own_low,
            dst_ref=lows.at[j],
            send_sem=ag_send.at[d - 1],
            recv_sem=ag_recv.at[j],
            device_id=(i, (j + d) % 16),
            device_id_type=MESH,
        )
        copy.start()
        shared.append(copy)
    lows[j] = total.astype(bf16)
    for d in range(1, 16):
        k = (j + d) % 16
        pltpu.make_async_remote_copy(
            src_ref=own_low,
            dst_ref=lows.at[k],
            send_sem=ag_send.at[d - 1],
            recv_sem=ag_recv.at[k],
            device_id=(i, k),
            device_id_type=MESH,
        ).wait_recv()

    def product(zz, xx):
        return dot(lows[row_of(zz, xx)], tokens)

    order = (2, 1, 3, 0)
    far = []
    for q, dz in enumerate(order):
        s_far[q] = product(zh + dz, x + 2).astype(bf16)
        far.append((
            copies(s_far.at[q, top], r_far_up.at[q], x_up),
            copies(s_far.at[q, bottom], r_far_down.at[q], x_down),
        ))
    near = []
    for q, dz in enumerate(order):
        value = product(zh + dz, x + 1)
        far[q][0].wait_recv()
        s_up[q, top] = (value[:half] + r_far_up[q].astype(f32)).astype(bf16)
        s_up[q, bottom] = value[half:].astype(bf16)
        a = copies(s_up.at[q], r_up.at[q], x_up)
        value = product(zh + dz, x + 3)
        far[q][1].wait_recv()
        s_down[q, top] = value[:half].astype(bf16)
        s_down[q, bottom] = (value[half:] + r_far_down[q].astype(f32)).astype(bf16)
        b = copies(s_down.at[q], r_down.at[q], x_down)
        near.append((a, b))
        own[q] = product(zh + dz, x)

    def joined(q):
        near[q][0].wait_recv()
        near[q][1].wait_recv()
        return own[q] + (r_up[q].astype(f32) + r_down[q].astype(f32))

    z_far[...] = joined(0).astype(bf16)
    za = copies(z_far.at[top], zr_far_up, z_next)
    zb = copies(z_far.at[bottom], zr_far_down, z_prev)
    value = joined(1)
    z_up[bottom] = value[half:].astype(bf16)
    za.wait_recv()
    z_up[top] = (value[:half] + zr_far_up[...].astype(f32)).astype(bf16)
    zc = copies(z_up, zr_up, z_next)
    value = joined(2)
    z_down[top] = value[:half].astype(bf16)
    zb.wait_recv()
    z_down[bottom] = (value[half:] + zr_far_down[...].astype(f32)).astype(bf16)
    zd = copies(z_down, zr_down, z_prev)
    value = joined(3)
    zc.wait_recv()
    zd.wait_recv()
    cor_ref[...] = (value + (zr_up[...].astype(f32) + zr_down[...].astype(f32))) * scale

    copies.drain()
    for s, copy in partials:
        pl.when(s != j)(copy.wait_send)
    for copy in shared:
        copy.wait_send()


def refresh(low, tokens, targets_t, scale):
    m, n = low.shape
    t = tokens.shape[0]
    sems = 4 + 16 + 16 + 4
    dma = pltpu.SemaphoreType.DMA

    def wide(*lead):
        return pltpu.VMEM((*lead, n), bf16)

    return pl.pallas_call(
        functools.partial(refresh_kernel, scale),
        out_shape=(jax.ShapeDtypeStruct((m, t), f32), jax.ShapeDtypeStruct((m, n), f32)),
        in_specs=[VMEM] * 3,
        out_specs=(VMEM, VMEM),
        scratch_shapes=[
            wide(16, m), pltpu.VMEM((16, m, t), f32), pltpu.VMEM((16, m, t), f32),
            pltpu.VMEM((m, t), bf16), pltpu.VMEM((16, m, t), bf16),
            wide(4, m), wide(4, m // 2), wide(4, m // 2), wide(4, m), wide(4, m), wide(4, m), wide(4, m),
            pltpu.VMEM((4, m, n), f32),
            wide(m), wide(m // 2), wide(m // 2), wide(m), wide(m), wide(m), wide(m),
            dma((sems,)), dma((sems,)), dma((16,)), dma((16,)), dma((15,)), dma((16,)),
        ],
        compiler_params=pltpu.CompilerParams(collective_id=1, has_side_effects=True, vmem_limit_bytes=32 << 20),
        cost_estimate=pl.CostEstimate(flops=10**9, bytes_accessed=200 * 10**6, transcendentals=0),
        name="refresh",
    )(low, tokens, targets_t)


def spread_panel(array, mine, axis):
    share = lax.psum_scatter(jnp.where(mine, array, jnp.zeros_like(array)), axis, scatter_dimension=0, tiled=True)
    return lax.all_gather(share, axis, axis=0, tiled=True)


def shards(panels, inverse, weight, tokens, targets):
    high = lax.Precision.HIGH
    i, j = lax.axis_index("row"), lax.axis_index("col")
    p = panels[0]
    packed = block_everywhere(panels, inverse)
    weight_slab = lax.psum(jnp.where(j == p, weight, jnp.zeros_like(weight)), "col")
    row_panel = spread_panel(inverse.astype(ROW_TYPE), i == p, "row").astype(f32)
    column = spread_panel(inverse.astype(COL_TYPE), j == p, "col").astype(f32)
    block_inverse = panel_inverse(packed)
    solved = jnp.dot(block_inverse, row_panel, precision=high, preferred_element_type=f32)
    pruned = weight - jnp.dot(weight_slab, solved, precision=high, preferred_element_type=f32)
    tokens_all = tokens.shape[0] * lax.axis_size("row")
    residual_t, correlation = refresh(
        pruned.astype(bf16), tokens, targets.T.astype(f32), 1.0 / math.sqrt(tokens_all)
    )
    new_inverse = inverse - jnp.dot(column, solved, precision=high, preferred_element_type=f32)
    return (new_inverse, pruned, residual_t.T, correlation)


ROW_TYPE = jnp.float32
COL_TYPE = jnp.float32


def solution(mesh):
    in_specs = (P(), P("row", "col"), P("row", "col"), P("row", "col"), P("row", "col"))
    out_specs = (P("row", "col"), P("row", "col"), P("row", "col"), P("row", "col"))
    return jax.shard_map(shards, mesh=mesh, in_specs=in_specs, out_specs=out_specs, check_vma=False)
```

```python
import functools
import math

import jax
import jax.numpy as jnp
from jax import lax
from jax.experimental import pallas as pl
from jax.experimental.pallas import tpu as pltpu
from jax.sharding import PartitionSpec as P

PW = 1024
NB = 128
MESH = pl.DeviceIdType.MESH
VMEM = pl.BlockSpec(memory_space=pltpu.VMEM)
f32 = jnp.float32
bf16 = jnp.bfloat16


def place():
    i, j = lax.axis_index("row"), lax.axis_index("col")
    return i, j, i // 4, i % 4, j // 4, (j // 2) % 2, j % 2


def row_of(zh, x):
    return (zh % 4) * 4 + x % 4


def col_of(y, zl, c):
    return ((y % 4) * 2 + zl % 2) * 2 + c % 2


class Copies:
    def __init__(self, send, recv):
        self.send, self.recv, self.made = send, recv, []

    def plan(self, src, dst, device):
        n = len(self.made)
        copy = pltpu.make_async_remote_copy(
            src_ref=src,
            dst_ref=dst,
            send_sem=self.send.at[n],
            recv_sem=self.recv.at[n],
            device_id=device,
            device_id_type=MESH,
        )
        self.made.append(copy)
        return copy

    def __call__(self, src, dst, device):
        copy = self.plan(src, dst, device)
        copy.start()
        return copy

    def drain(self):
        for copy in self.made:
            copy.wait_send()


def meet(devices):
    barrier = pltpu.get_barrier_semaphore()
    for device in devices:
        pl.semaphore_signal(barrier, inc=1, device_id=device, device_id_type=MESH)
    pl.semaphore_wait(barrier, len(devices))


PR, PC = 32, 1152
CB = 136
CT = 72


def at(start, size):
    return pl.ds(pl.multiple_of(start, 8), size)


def fill(dst, start, rows, value):
    @pl.loop(0, rows // 8)
    def _(t):
        r = pl.multiple_of(t * 8, 8)
        dst[at(start + r, 8), :] = value(r)


def front_kernel(
    p_ref, h_ref, w_ref, a, rows, cw, pruned_ref, low_ref,
    hw, pack, chunk, got, mine, zgot, packed, piv,
    ra, sb, rb, acc, rz, sz, rzn,
    rc, m0, ryu, ryd, sy, ry, acc_c, rcz,
    local, send1, recv1, send, recv,
):
    i, j, zh, x, y, zl, c = place()
    p = p_ref[0]
    loads = [
        pltpu.make_async_copy(h_ref, hw.at[pl.ds(0, PW)], local.at[9]),
        pltpu.make_async_copy(w_ref, hw.at[pl.ds(PW, 64)], local.at[10]),
    ]
    for load in loads:
        load.start()
    xs = [(row_of(zh, x + d), j) for d in (1, 2, 3)]
    zs = [(row_of(zh + d, x), j) for d in (1, 2, 3)]
    meet([(i, (j + d) % 16) for d in range(1, 16)] + xs + zs)
    x_up, x_down, z_next, z_prev = xs[0], xs[2], zs[0], zs[2]
    y_up, y_down = (i, col_of(y + 1, zl, c)), (i, col_of(y + 3, zl, c))
    across, peer = (i, col_of(y, zl + 1, c)), (i, col_of(y, zl, c + 1))
    copies = Copies(send, recv)

    scatter = [
        pltpu.make_async_remote_copy(
            src_ref=pack.at[at(((j + d) % 16) * PR, PR)],
            dst_ref=chunk,
            send_sem=send1.at[d - 1],
            recv_sem=recv1,
            device_id=(i, (j + d) % 16),
            device_id_type=MESH,
        )
        for d in range(1, 16)
    ]

    @pl.when(i == j)
    def _():
        loads = []
        for g in range(4):
            r = pl.ds(128 * g, 128)
            m, n = 128 * (g + 1), 128 * (8 - g)
            loads.append(pltpu.make_async_copy(h_ref.at[r, pl.ds(0, m)], pack.at[r, pl.ds(0, m)], local.at[2 * g]))
            far = pl.ds(128 * (7 - g), 128)
            loads.append(pltpu.make_async_copy(h_ref.at[far, pl.ds(0, n)], pack.at[r, pl.ds(m, n)], local.at[2 * g + 1]))
        for load in loads:
            load.start()
        for load in loads:
            load.wait()
        for copy in scatter:
            copy.start()
        own = pltpu.make_async_copy(pack.at[at(j * PR, PR)], chunk, local.at[8])
        own.start()
        own.wait()

    for load in loads:
        load.wait()

    own_row = i == p
    far = ((x + 2) % 4) * 256
    ra_up = copies(hw.at[at(far, 128)], ra.at[0], x_up)
    ra_down = copies(hw.at[at(far + 128, 128)], ra.at[1], x_down)
    rb_up = copies.plan(sb.at[0], rb.at[0], x_up)
    rb_down = copies.plan(sb.at[1], rb.at[1], x_down)
    far = ((zh + 2) % 4) * 64
    za_up = copies.plan(acc.at[at(far, 32)], rz.at[0], z_next)
    za_down = copies.plan(acc.at[at(far + 32, 32)], rz.at[1], z_prev)
    zb_up = copies.plan(sz.at[0], rzn.at[0], z_next)
    zb_down = copies.plan(sz.at[1], rzn.at[1], z_prev)

    def chunk_at(k):
        return x * 256 + ((zh + k) % 4) * 64

    def block_at(k):
        return ((x + k) % 4) * 256

    def same(ref, start, size, device):
        return copies.plan(ref.at[at(start, size)], ref.at[at(start, size)], device)

    ga = [same(rows, chunk_at(0), 64, z_next), same(rows, chunk_at(0), 64, z_prev)]
    gb = [same(rows, chunk_at(3), 32, z_next), same(rows, chunk_at(1) + 32, 32, z_prev)]
    gx = [same(rows, block_at(0), 256, x_up), same(rows, block_at(0), 256, x_down)]
    gy = [same(rows, block_at(3), 128, x_up), same(rows, block_at(1) + 128, 128, x_down)]

    def held(r):
        return jnp.where(own_row, hw[at(r, 8), :], 0.0)

    def rows_near():
        ra_up.wait_recv()
        ra_down.wait_recv()
        before = row_of(zh, x + 3) == p
        after = row_of(zh, x + 1) == p
        up, down = block_at(1), block_at(3)
        fill(sb.at[0], 0, 128, lambda r: held(up + r) + jnp.where(before, ra[0, at(r, 8), :], 0.0))
        fill(sb.at[0], 128, 128, lambda r: held(up + 128 + r))
        rb_up.start()
        fill(sb.at[1], 0, 128, lambda r: held(down + r))
        fill(sb.at[1], 128, 128, lambda r: held(down + 128 + r) + jnp.where(after, ra[1, at(r, 8), :], 0.0))
        rb_down.start()

    def rows_z_far():
        rb_up.wait_recv()
        rb_down.wait_recv()
        fill(acc, 0, 256, lambda r: held(block_at(0) + r) + (rb[0, at(r, 8), :] + rb[1, at(r, 8), :]))
        za_up.start()
        za_down.start()

    def rows_z_near():
        za_up.wait_recv()
        za_down.wait_recv()
        up, down = ((zh + 1) % 4) * 64, ((zh + 3) % 4) * 64
        fill(sz.at[0], 0, 32, lambda r: acc[at(up + r, 8), :] + rz[0, at(r, 8), :])
        fill(sz.at[0], 32, 32, lambda r: acc[at(up + 32 + r, 8), :])
        zb_up.start()
        fill(sz.at[1], 0, 32, lambda r: acc[at(down + r, 8), :])
        fill(sz.at[1], 32, 32, lambda r: acc[at(down + 32 + r, 8), :] + rz[1, at(r, 8), :])
        zb_down.start()

    def rows_final():
        zb_up.wait_recv()
        zb_down.wait_recv()
        mid = zh * 64
        fill(rows, chunk_at(0), 64, lambda r: acc[at(mid + r, 8), :] + (rzn[0, at(r, 8), :] + rzn[1, at(r, 8), :]))
        for copy in ga:
            copy.start()

    def handed(waits, starts):
        for copy in waits:
            copy.wait_recv()
        for copy in starts:
            copy.start()

    ca = copies(hw.at[at((1 - c) * 4 * CB, 4 * CB)], rc, peer)
    far = ((y + 2) % 4) * CB
    ya_up = copies.plan(m0.at[at(far, CT)], ryu, y_up)
    ya_down = copies.plan(m0.at[at(far + CT, CB - CT)], ryd, y_down)
    yb_up = copies.plan(sy.at[0], ry.at[0], y_up)
    yb_down = copies.plan(sy.at[1], ry.at[1], y_down)
    cz = copies.plan(acc_c, rcz, across)

    def col_at(k):
        return c * 4 * CB + ((y + k) % 4) * CB

    cy = [same(cw, col_at(0), CB, y_up), same(cw, col_at(0), CB, y_down)]
    cy2 = [same(cw, col_at(3), CT, y_up), same(cw, col_at(1) + CT, CB - CT, y_down)]
    cc = [same(cw, col_at(k), CB, peer) for k in range(4)]

    def cols_far():
        ca.wait_recv()
        own, other = j == p, col_of(y, zl, c + 1) == p
        base = c * 4 * CB
        fill(m0, 0, 4 * CB, lambda r: jnp.where(own, hw[at(base + r, 8), :], 0.0) + jnp.where(other, rc[at(r, 8), :], 0.0))
        ya_up.start()
        ya_down.start()

    def cols_near():
        ya_up.wait_recv()
        ya_down.wait_recv()
        up, down = ((y + 1) % 4) * CB, ((y + 3) % 4) * CB
        fill(sy.at[0], 0, CT, lambda r: m0[at(up + r, 8), :] + ryu[at(r, 8), :])
        fill(sy.at[0], CT, CB - CT, lambda r: m0[at(up + CT + r, 8), :])
        yb_up.start()
        fill(sy.at[1], 0, CT, lambda r: m0[at(down + r, 8), :])
        fill(sy.at[1], CT, CB - CT, lambda r: m0[at(down + CT + r, 8), :] + ryd[at(r, 8), :])
        yb_down.start()

    def cols_across():
        yb_up.wait_recv()
        yb_down.wait_recv()
        mid = y * CB
        fill(acc_c, 0, CB, lambda r: m0[at(mid + r, 8), :] + (ry[0, at(r, 8), :] + ry[1, at(r, 8), :]))
        cz.start()

    def cols_final():
        cz.wait_recv()
        fill(cw, col_at(0), CB, lambda r: acc_c[at(r, 8), :] + rcz[at(r, 8), :])
        for copy in cy + cc[:1]:
            copy.start()

    @pl.when(i != j)
    def _():
        scatter[0].wait_recv()

    def piece(k):
        return at((k % 4) * 8, 8)

    firsts = [copies(chunk.at[piece(x + d)], got.at[d - 1], xs[d - 1]) for d in (1, 2, 3)]
    part = jnp.where(own_row, chunk[piece(x), :], 0.0)
    for d in (1, 2, 3):
        firsts[d - 1].wait_recv()
        part = part + jnp.where(row_of(zh, x - d + 4) == p, got[d - 1], 0.0)
    mine[...] = part
    seconds = [copies(mine, zgot.at[d - 1], zs[d - 1]) for d in (1, 2, 3)]
    for d in (1, 2, 3):
        seconds[d - 1].wait_recv()
        part = part + zgot[d - 1]
    packed[j, piece(x), :] = part
    thirds = [copies(packed.at[j, piece(x)], packed.at[j, piece(x)], xs[d - 1]) for d in (1, 2, 3)]
    for copy in thirds:
        copy.wait_recv()
    rows_near()
    gather_cols(copies, packed, packed, PR)

    stages = [
        (rows_z_far, cols_far),
        (rows_z_near, cols_near),
        (rows_final, cols_across),
        (lambda: handed(ga, gb), cols_final),
        (lambda: handed(gb, gx), lambda: handed(cy, cy2 + [cc[3], cc[1]])),
        (lambda: handed(cy2, [cc[2]]),),
        (lambda: handed(gx, gy),),
        (lambda: handed(cc, []),),
    ]

    for g in range(4):
        for r, start in ((g, 0), (7 - g, 128 * (g + 1))):
            for q in range(r + 1):
                lanes = pl.ds(start + 128 * q, 128)
                tile = jnp.concatenate([packed[4 * g + m, :, lanes] for m in range(4)], axis=0)
                a[pl.ds(128 * r, 128), pl.ds(128 * q, 128)] = tile
                if q < r:
                    a[pl.ds(128 * q, 128), pl.ds(128 * r, 128)] = tile.T
    eye = (lax.broadcasted_iota(jnp.int32, (NB, NB), 0) == lax.broadcasted_iota(jnp.int32, (NB, NB), 1)).astype(f32)

    def step(kb, _):
        for n, stage in enumerate(stages):

            @pl.when(kb == n)
            def _():
                for part in stage:
                    part()

        sweep(a, piv, eye, kb)
        return 0

    lax.fori_loop(0, PW // NB, step, 0)
    handed(gy, [])

    lead = dot3(cw[pl.ds(PW, 64), :], a[...])
    for t in range(4):
        lanes = pl.ds(256 * t, 256)
        value = hw[pl.ds(PW, 64), lanes] - dot3(lead, rows[:, lanes])
        pruned_ref[:, lanes] = value
        low_ref[:, lanes] = value.astype(bf16)

    copies.drain()

    @pl.when(i == j)
    def _():
        for copy in scatter:
            copy.wait_send()


def sweep(a, piv, eye, kb):
    n = PW
    here = pl.ds(pl.multiple_of(kb * NB, NB), NB)
    blk = [a[pl.ds(pl.multiple_of(kb * NB + 8 * w, 8), 8), here] for w in range(NB // 8)]
    inv = pivot_inverse(blk)
    for w in range(NB // 8):
        piv[8 * w : 8 * w + 8, :] = inv[w]
    a[here, here] = eye
    u = dot3(piv[...], a[here, :])
    uh, ul = split(u)
    a[here, here] = -eye
    ch, cl = split(a[:, here])
    a[here, :] = jnp.zeros((NB, n), f32)
    a[:, here] = jnp.zeros((n, NB), f32)
    uk = jnp.concatenate([uh, ul, uh], axis=0)
    ck = jnp.concatenate([ch, ch, cl], axis=1)
    for t in range(n // 256):
        r = slice(256 * t, 256 * t + 256)
        a[r, :] = a[r, :] - dot(ck[r, :], uk)


def front(panels, inverse, weight):
    sems = 9 + 25 + 16 + 14
    dma = pltpu.SemaphoreType.DMA

    def buf(*shape):
        return pltpu.VMEM((*shape, PW), f32)

    def out(*shape):
        return jax.ShapeDtypeStruct(shape, f32)

    return pl.pallas_call(
        front_kernel,
        out_shape=(out(PW, PW), out(PW, PW), out(8 * CB, PW), out(64, PW), jax.ShapeDtypeStruct((64, PW), bf16)),
        in_specs=[pl.BlockSpec(memory_space=pltpu.SMEM)] + [pl.BlockSpec(memory_space=pl.ANY)] * 2,
        out_specs=(VMEM,) * 5,
        scratch_shapes=[
            buf(8 * CB),
            pltpu.VMEM((16 * PR, PC), f32),
            pltpu.VMEM((PR, PC), f32),
            pltpu.VMEM((3, 8, PC), f32),
            pltpu.VMEM((8, PC), f32),
            pltpu.VMEM((3, 8, PC), f32),
            pltpu.VMEM((16, PR, PC), f32),
            pltpu.VMEM((NB, NB), f32),
            buf(2, 128), buf(2, 256), buf(2, 256), buf(256), buf(2, 32), buf(2, 64), buf(2, 64),
            buf(4 * CB), buf(4 * CB), buf(CT), buf(CB - CT), buf(2, CB), buf(2, CB), buf(CB), buf(CB),
            dma((11,)), dma((15,)), dma, dma((sems,)), dma((sems,)),
        ],
        compiler_params=pltpu.CompilerParams(collective_id=0, has_side_effects=True, vmem_limit_bytes=60 << 20),
        cost_estimate=pl.CostEstimate(flops=60 * 10**9, bytes_accessed=400 * 10**6, transcendentals=0),
        name="front",
    )(panels, inverse, weight)


def gather_cols(copies, first, out, rows):
    i, j, zh, x, y, zl, c = place()
    h = rows // 2
    ups, downs, cores = [], [], []
    across = copies(first.at[j], out.at[j], (i, col_of(y, zl + 1, c)))
    up, down = (i, col_of(y + 1, zl, c)), (i, col_of(y + 3, zl, c))
    peer = (i, col_of(y, zl, c + 1))
    for t in (0, 1):
        src = first if t == 0 else out
        if t == 1:
            across.wait_recv()
        s = col_of(y, zl + t, c)
        ups.append(copies(src.at[s], out.at[s], up))
        downs.append(copies(src.at[s], out.at[s], down))
        cores.append(copies(src.at[s], out.at[s], peer))
    halves = []
    for t in (0, 1):
        ups[t].wait_recv()
        s = col_of(y + 3, zl + t, c)
        halves.append(copies(out.at[s, pl.ds(0, h)], out.at[s, pl.ds(0, h)], up))
        cores.append(copies(out.at[s], out.at[s], peer))
        downs[t].wait_recv()
        s = col_of(y + 1, zl + t, c)
        halves.append(copies(out.at[s, pl.ds(h, h)], out.at[s, pl.ds(h, h)], down))
        cores.append(copies(out.at[s], out.at[s], peer))
    for t in (0, 1):
        halves[2 * t].wait_recv()
        halves[2 * t + 1].wait_recv()
        s = col_of(y + 2, zl + t, c)
        cores.append(copies(out.at[s], out.at[s], peer))
    for copy in cores:
        copy.wait_recv()


def split(x):
    hi = x.astype(bf16)
    return hi, (x - hi.astype(f32)).astype(bf16)


def dot(a, b):
    return jnp.dot(a, b, preferred_element_type=f32)


def dot3(a, b):
    ah, al = split(a)
    bh, bl = split(b)
    return dot(ah, bh) + (dot(ah, bl) + dot(al, bh))


def pivot_inverse(rows):
    lane = lax.broadcasted_iota(jnp.int32, (8, NB), 1)
    sub = lax.broadcasted_iota(jnp.int32, (8, NB), 0)
    lane1 = lax.broadcasted_iota(jnp.int32, (1, NB), 1)
    rows = list(rows)
    for k in range(0, NB, 2):
        v, s = k // 8, k % 8
        c0 = [jnp.broadcast_to(r[:, k : k + 1], (8, NB)) for r in rows]
        c1 = [jnp.broadcast_to(r[:, k + 1 : k + 2], (8, NB)) for r in rows]
        r0, r1 = rows[v][s : s + 1, :], rows[v][s + 1 : s + 2, :]
        p00, p01 = c0[v][s : s + 1, :], c1[v][s : s + 1, :]
        p10, p11 = c0[v][s + 1 : s + 2, :], c1[v][s + 1 : s + 2, :]
        scale = 1.0 / (p00 * p11 - p01 * p10)
        e0, e1 = lane1 == k, lane1 == k + 1
        r0 = jnp.where(e0, 1.0, jnp.where(e1, 0.0, r0))
        r1 = jnp.where(e1, 1.0, jnp.where(e0, 0.0, r1))
        u0 = jnp.broadcast_to((p11 * scale) * r0 - (p01 * scale) * r1, (8, NB))
        u1 = jnp.broadcast_to((p00 * scale) * r1 - (p10 * scale) * r0, (8, NB))
        cols = (lane == k) | (lane == k + 1)
        for w in range(NB // 8):
            base = jnp.where(cols, 0.0, rows[w]) - c0[w] * u0 - c1[w] * u1
            if w == v:
                base = jnp.where(sub == s, u0, jnp.where(sub == s + 1, u1, base))
            rows[w] = base
    return rows


def refresh_kernel(
    scale, low_ref, tok_ref, tgt_ref, res_ref, cor_ref, every, part, heard, own_low, lows,
    s_far, r_far_up, r_far_down, s_up, s_down, r_up, r_down, own,
    z_far, zr_far_up, zr_far_down, z_up, z_down, zr_up, zr_down,
    send, recv, rs_send, rs_recv, ag_send, ag_recv,
):
    i, j, zh, x, y, zl, c = place()
    x_up, x_down = (row_of(zh, x + 1), j), (row_of(zh, x + 3), j)
    z_next, z_prev = (row_of(zh + 1, x), j), (row_of(zh + 3, x), j)
    meet([(i, (j + d) % 16) for d in range(1, 16)] + [x_up, x_down, z_next, z_prev])
    copies = Copies(send, recv)
    tokens = tok_ref[...]
    half = low_ref.shape[0] // 2
    top, bottom = pl.ds(0, half), pl.ds(half, half)

    partials = []

    def use(s, block):
        value = lax.dot_general(block[...], tokens, (((1,), (1,)), ((), ())), preferred_element_type=f32)
        part[s] = value
        copy = pltpu.make_async_remote_copy(
            src_ref=part.at[s],
            dst_ref=heard.at[j],
            send_sem=rs_send.at[s],
            recv_sem=rs_recv.at[j],
            device_id=(i, s),
            device_id_type=MESH,
        )
        pl.when(s != j)(copy.start)
        partials.append((s, copy))

    def spread(s, block):
        return s, copies(block, every.at[s], x_up), copies(block, every.at[s], x_down)

    zn = copies(low_ref, every.at[i], z_next)
    zp = copies(low_ref, every.at[i], z_prev)
    sent = [spread(i, low_ref)]
    use(i, low_ref)
    zn.wait_recv()
    s = row_of(zh + 3, x)
    z1 = copies(every.at[s, top], every.at[s, top], z_next)
    sent.append(spread(s, every.at[s]))
    zp.wait_recv()
    s = row_of(zh + 1, x)
    z2 = copies(every.at[s, bottom], every.at[s, bottom], z_prev)
    sent.append(spread(s, every.at[s]))
    use(row_of(zh + 3, x), every.at[row_of(zh + 3, x)])
    use(s, every.at[s])
    z1.wait_recv()
    z2.wait_recv()
    s = row_of(zh + 2, x)
    sent.append(spread(s, every.at[s]))
    use(s, every.at[s])
    lasts = []
    for dz, (_, up, down) in zip((0, 3, 1, 2), sent):
        up.wait_recv()
        s = row_of(zh + dz, x + 3)
        a = copies(every.at[s, top], every.at[s, top], x_up)
        use(s, every.at[s])
        down.wait_recv()
        s = row_of(zh + dz, x + 1)
        b = copies(every.at[s, bottom], every.at[s, bottom], x_down)
        use(s, every.at[s])
        lasts.append((dz, a, b))
    for dz, a, b in lasts:
        a.wait_recv()
        b.wait_recv()
        s = row_of(zh + dz, x + 2)
        use(s, every.at[s])

    total = part[j] - tgt_ref[...]
    for d in range(1, 16):
        k = (j + d) % 16
        pltpu.make_async_remote_copy(
            src_ref=part.at[k],
            dst_ref=heard.at[k],
            send_sem=rs_send.at[k],
            recv_sem=rs_recv.at[k],
            device_id=(i, k),
            device_id_type=MESH,
        ).wait_recv()
        total = total + heard[k]
    res_ref[...] = total
    own_low[...] = total.astype(bf16)

    shared = []
    for d in range(1, 16):
        copy = pltpu.make_async_remote_copy(
            src_ref=own_low,
            dst_ref=lows.at[j],
            send_sem=ag_send.at[d - 1],
            recv_sem=ag_recv.at[j],
            device_id=(i, (j + d) % 16),
            device_id_type=MESH,
        )
        copy.start()
        shared.append(copy)
    lows[j] = total.astype(bf16)
    for d in range(1, 16):
        k = (j + d) % 16
        pltpu.make_async_remote_copy(
            src_ref=own_low,
            dst_ref=lows.at[k],
            send_sem=ag_send.at[d - 1],
            recv_sem=ag_recv.at[k],
            device_id=(i, k),
            device_id_type=MESH,
        ).wait_recv()

    def product(zz, xx):
        return dot(lows[row_of(zz, xx)], tokens)

    order = (2, 1, 3, 0)
    far = []
    for q, dz in enumerate(order):
        s_far[q] = product(zh + dz, x + 2).astype(bf16)
        far.append((
            copies(s_far.at[q, top], r_far_up.at[q], x_up),
            copies(s_far.at[q, bottom], r_far_down.at[q], x_down),
        ))
    near = []
    for q, dz in enumerate(order):
        value = product(zh + dz, x + 1)
        far[q][0].wait_recv()
        s_up[q, top] = (value[:half] + r_far_up[q].astype(f32)).astype(bf16)
        s_up[q, bottom] = value[half:].astype(bf16)
        a = copies(s_up.at[q], r_up.at[q], x_up)
        value = product(zh + dz, x + 3)
        far[q][1].wait_recv()
        s_down[q, top] = value[:half].astype(bf16)
        s_down[q, bottom] = (value[half:] + r_far_down[q].astype(f32)).astype(bf16)
        b = copies(s_down.at[q], r_down.at[q], x_down)
        near.append((a, b))
        own[q] = product(zh + dz, x)

    def joined(q):
        near[q][0].wait_recv()
        near[q][1].wait_recv()
        return own[q] + (r_up[q].astype(f32) + r_down[q].astype(f32))

    z_far[...] = joined(0).astype(bf16)
    za = copies(z_far.at[top], zr_far_up, z_next)
    zb = copies(z_far.at[bottom], zr_far_down, z_prev)
    value = joined(1)
    z_up[bottom] = value[half:].astype(bf16)
    za.wait_recv()
    z_up[top] = (value[:half] + zr_far_up[...].astype(f32)).astype(bf16)
    zc = copies(z_up, zr_up, z_next)
    value = joined(2)
    z_down[top] = value[:half].astype(bf16)
    zb.wait_recv()
    z_down[bottom] = (value[half:] + zr_far_down[...].astype(f32)).astype(bf16)
    zd = copies(z_down, zr_down, z_prev)
    value = joined(3)
    zc.wait_recv()
    zd.wait_recv()
    cor_ref[...] = (value + (zr_up[...].astype(f32) + zr_down[...].astype(f32))) * scale

    copies.drain()
    for s, copy in partials:
        pl.when(s != j)(copy.wait_send)
    for copy in shared:
        copy.wait_send()


def refresh(low, tokens, targets_t, scale):
    m, n = low.shape
    t = tokens.shape[0]
    sems = 4 + 16 + 16 + 4
    dma = pltpu.SemaphoreType.DMA

    def wide(*lead):
        return pltpu.VMEM((*lead, n), bf16)

    return pl.pallas_call(
        functools.partial(refresh_kernel, scale),
        out_shape=(jax.ShapeDtypeStruct((m, t), f32), jax.ShapeDtypeStruct((m, n), f32)),
        in_specs=[VMEM] * 3,
        out_specs=(VMEM, VMEM),
        scratch_shapes=[
            wide(16, m), pltpu.VMEM((16, m, t), f32), pltpu.VMEM((16, m, t), f32),
            pltpu.VMEM((m, t), bf16), pltpu.VMEM((16, m, t), bf16),
            wide(4, m), wide(4, m // 2), wide(4, m // 2), wide(4, m), wide(4, m), wide(4, m), wide(4, m),
            pltpu.VMEM((4, m, n), f32),
            wide(m), wide(m // 2), wide(m // 2), wide(m), wide(m), wide(m), wide(m),
            dma((sems,)), dma((sems,)), dma((16,)), dma((16,)), dma((15,)), dma((16,)),
        ],
        compiler_params=pltpu.CompilerParams(collective_id=1, has_side_effects=True, vmem_limit_bytes=32 << 20),
        cost_estimate=pl.CostEstimate(flops=10**9, bytes_accessed=200 * 10**6, transcendentals=0),
        name="refresh",
    )(low, tokens, targets_t)


def shards(panels, inverse, weight, tokens, targets):
    high = lax.Precision.HIGH
    block_inverse, row_panel, columns, pruned, low = front(panels, inverse, weight)
    token_count = tokens.shape[0] * lax.axis_size("row")
    residual_t, correlation = refresh(low, tokens, targets.T.astype(f32), 1.0 / math.sqrt(token_count))
    solved = jnp.dot(block_inverse, row_panel, precision=high, preferred_element_type=f32)
    new_inverse = inverse - jnp.dot(columns[:PW], solved, precision=high, preferred_element_type=f32)
    return (new_inverse, pruned, residual_t.T, correlation)


def solution(mesh):
    in_specs = (P(), P("row", "col"), P("row", "col"), P("row", "col"), P("row", "col"))
    out_specs = (P("row", "col"), P("row", "col"), P("row", "col"), P("row", "col"))
    return jax.shard_map(shards, mesh=mesh, in_specs=in_specs, out_specs=out_specs, check_vma=False)
```

```python
import functools
import math

import jax
import jax.numpy as jnp
from jax import lax
from jax.experimental import pallas as pl
from jax.experimental.pallas import tpu as pltpu
from jax.sharding import PartitionSpec as P

PW = 1024
NB = 128
MESH = pl.DeviceIdType.MESH
VMEM = pl.BlockSpec(memory_space=pltpu.VMEM)
f32 = jnp.float32
bf16 = jnp.bfloat16


def place():
    i, j = lax.axis_index("row"), lax.axis_index("col")
    return i, j, i // 4, i % 4, j // 4, (j // 2) % 2, j % 2


def row_of(zh, x):
    return (zh % 4) * 4 + x % 4


def col_of(y, zl, c):
    return ((y % 4) * 2 + zl % 2) * 2 + c % 2


class Copies:
    def __init__(self, send, recv):
        self.send, self.recv, self.made = send, recv, []

    def plan(self, src, dst, device):
        n = len(self.made)
        copy = pltpu.make_async_remote_copy(
            src_ref=src,
            dst_ref=dst,
            send_sem=self.send.at[n],
            recv_sem=self.recv.at[n],
            device_id=device,
            device_id_type=MESH,
        )
        self.made.append(copy)
        return copy

    def __call__(self, src, dst, device):
        copy = self.plan(src, dst, device)
        copy.start()
        return copy

    def drain(self):
        for copy in self.made:
            copy.wait_send()


def meet(devices):
    barrier = pltpu.get_barrier_semaphore()
    for device in devices:
        pl.semaphore_signal(barrier, inc=1, device_id=device, device_id_type=MESH)
    pl.semaphore_wait(barrier, len(devices))


PR, PC = 32, 1152
CB = 136
CT = 72


def at(start, size):
    return pl.ds(pl.multiple_of(start, 8), size)


def fill(dst, start, rows, value):
    @pl.loop(0, rows // 8)
    def _(t):
        r = pl.multiple_of(t * 8, 8)
        dst[at(start + r, 8), :] = value(r)


def front_kernel(
    p_ref, h_ref, w_ref, inv_out, rows_out, cw_out, pruned_ref, low_ref,
    a, rows, cw, us, hw, pack, chunk, got, mine, zgot, packed, piv,
    ra, sb, rb, acc, rz, sz, rzn,
    rc, m0, ryu, ryd, sy, ry, acc_c, rcz,
    local, send1, recv1, send, recv,
):
    i, j, zh, x, y, zl, c = place()
    p = p_ref[0]
    loads = [
        pltpu.make_async_copy(h_ref, hw.at[pl.ds(0, PW)], local.at[9]),
        pltpu.make_async_copy(w_ref, hw.at[pl.ds(PW, 64)], local.at[10]),
    ]
    for load in loads:
        load.start()
    xs = [(row_of(zh, x + d), j) for d in (1, 2, 3)]
    zs = [(row_of(zh + d, x), j) for d in (1, 2, 3)]
    meet([(i, (j + d) % 16) for d in range(1, 16)] + xs + zs)
    x_up, x_down, z_next, z_prev = xs[0], xs[2], zs[0], zs[2]
    y_up, y_down = (i, col_of(y + 1, zl, c)), (i, col_of(y + 3, zl, c))
    across, peer = (i, col_of(y, zl + 1, c)), (i, col_of(y, zl, c + 1))
    copies = Copies(send, recv)

    scatter = [
        pltpu.make_async_remote_copy(
            src_ref=pack.at[at(((j + d) % 16) * PR, PR)],
            dst_ref=chunk,
            send_sem=send1.at[d - 1],
            recv_sem=recv1,
            device_id=(i, (j + d) % 16),
            device_id_type=MESH,
        )
        for d in range(1, 16)
    ]

    @pl.when(i == j)
    def _():
        loads = []
        for g in range(4):
            r = pl.ds(128 * g, 128)
            m, n = 128 * (g + 1), 128 * (8 - g)
            loads.append(pltpu.make_async_copy(h_ref.at[r, pl.ds(0, m)], pack.at[r, pl.ds(0, m)], local.at[2 * g]))
            far = pl.ds(128 * (7 - g), 128)
            loads.append(pltpu.make_async_copy(h_ref.at[far, pl.ds(0, n)], pack.at[r, pl.ds(m, n)], local.at[2 * g + 1]))
        for load in loads:
            load.start()
        for load in loads:
            load.wait()
        for copy in scatter:
            copy.start()
        own = pltpu.make_async_copy(pack.at[at(j * PR, PR)], chunk, local.at[8])
        own.start()
        own.wait()

    for load in loads:
        load.wait()

    own_row = i == p
    far = ((x + 2) % 4) * 256
    ra_up = copies(hw.at[at(far, 128)], ra.at[0], x_up)
    ra_down = copies(hw.at[at(far + 128, 128)], ra.at[1], x_down)
    rb_up = copies.plan(sb.at[0], rb.at[0], x_up)
    rb_down = copies.plan(sb.at[1], rb.at[1], x_down)
    far = ((zh + 2) % 4) * 64
    za_up = copies.plan(acc.at[at(far, 32)], rz.at[0], z_next)
    za_down = copies.plan(acc.at[at(far + 32, 32)], rz.at[1], z_prev)
    zb_up = copies.plan(sz.at[0], rzn.at[0], z_next)
    zb_down = copies.plan(sz.at[1], rzn.at[1], z_prev)

    def chunk_at(k):
        return x * 256 + ((zh + k) % 4) * 64

    def block_at(k):
        return ((x + k) % 4) * 256

    def same(ref, start, size, device):
        return copies.plan(ref.at[at(start, size)], ref.at[at(start, size)], device)

    ga = [same(rows, chunk_at(0), 64, z_next), same(rows, chunk_at(0), 64, z_prev)]
    gb = [same(rows, chunk_at(3), 32, z_next), same(rows, chunk_at(1) + 32, 32, z_prev)]

    def far_chunk(k, n):
        return ((x + n) % 4) * 256 + ((zh + k) % 4) * 64

    gx = [[same(rows, chunk_at(k), 64, x_up), same(rows, chunk_at(k), 64, x_down)] for k in (0, 1, 3, 2)]
    gy = [
        [same(rows, far_chunk(k, 3), 32, x_up), same(rows, far_chunk(k, 1) + 32, 32, x_down)] for k in (0, 1, 3, 2)
    ]

    def held(r):
        return jnp.where(own_row, hw[at(r, 8), :], 0.0)

    def rows_near():
        ra_up.wait_recv()
        ra_down.wait_recv()
        before = row_of(zh, x + 3) == p
        after = row_of(zh, x + 1) == p
        up, down = block_at(1), block_at(3)
        fill(sb.at[0], 0, 128, lambda r: held(up + r) + jnp.where(before, ra[0, at(r, 8), :], 0.0))
        fill(sb.at[0], 128, 128, lambda r: held(up + 128 + r))
        rb_up.start()
        fill(sb.at[1], 0, 128, lambda r: held(down + r))
        fill(sb.at[1], 128, 128, lambda r: held(down + 128 + r) + jnp.where(after, ra[1, at(r, 8), :], 0.0))
        rb_down.start()

    def rows_z_far():
        rb_up.wait_recv()
        rb_down.wait_recv()
        fill(acc, 0, 256, lambda r: held(block_at(0) + r) + (rb[0, at(r, 8), :] + rb[1, at(r, 8), :]))
        za_up.start()
        za_down.start()

    def rows_z_near():
        za_up.wait_recv()
        za_down.wait_recv()
        up, down = ((zh + 1) % 4) * 64, ((zh + 3) % 4) * 64
        fill(sz.at[0], 0, 32, lambda r: acc[at(up + r, 8), :] + rz[0, at(r, 8), :])
        fill(sz.at[0], 32, 32, lambda r: acc[at(up + 32 + r, 8), :])
        zb_up.start()
        fill(sz.at[1], 0, 32, lambda r: acc[at(down + r, 8), :])
        fill(sz.at[1], 32, 32, lambda r: acc[at(down + 32 + r, 8), :] + rz[1, at(r, 8), :])
        zb_down.start()

    def rows_final():
        zb_up.wait_recv()
        zb_down.wait_recv()
        mid = zh * 64
        fill(rows, chunk_at(0), 64, lambda r: acc[at(mid + r, 8), :] + (rzn[0, at(r, 8), :] + rzn[1, at(r, 8), :]))
        for copy in ga + gx[0]:
            copy.start()

    def handed(waits, starts):
        for copy in waits:
            copy.wait_recv()
        for copy in starts:
            copy.start()

    ca = copies(hw.at[at((1 - c) * 4 * CB, 4 * CB)], rc, peer)
    far = ((y + 2) % 4) * CB
    ya_up = copies.plan(m0.at[at(far, CT)], ryu, y_up)
    ya_down = copies.plan(m0.at[at(far + CT, CB - CT)], ryd, y_down)
    yb_up = copies.plan(sy.at[0], ry.at[0], y_up)
    yb_down = copies.plan(sy.at[1], ry.at[1], y_down)
    cz = copies.plan(acc_c, rcz, across)

    def col_at(k):
        return c * 4 * CB + ((y + k) % 4) * CB

    cy = [same(cw, col_at(0), CB, y_up), same(cw, col_at(0), CB, y_down)]
    cy2 = [same(cw, col_at(3), CT, y_up), same(cw, col_at(1) + CT, CB - CT, y_down)]
    cc = [same(cw, col_at(k), CB, peer) for k in range(4)]

    def cols_far():
        ca.wait_recv()
        own, other = j == p, col_of(y, zl, c + 1) == p
        base = c * 4 * CB
        fill(m0, 0, 4 * CB, lambda r: jnp.where(own, hw[at(base + r, 8), :], 0.0) + jnp.where(other, rc[at(r, 8), :], 0.0))
        ya_up.start()
        ya_down.start()

    def cols_near():
        ya_up.wait_recv()
        ya_down.wait_recv()
        up, down = ((y + 1) % 4) * CB, ((y + 3) % 4) * CB
        fill(sy.at[0], 0, CT, lambda r: m0[at(up + r, 8), :] + ryu[at(r, 8), :])
        fill(sy.at[0], CT, CB - CT, lambda r: m0[at(up + CT + r, 8), :])
        yb_up.start()
        fill(sy.at[1], 0, CT, lambda r: m0[at(down + r, 8), :])
        fill(sy.at[1], CT, CB - CT, lambda r: m0[at(down + CT + r, 8), :] + ryd[at(r, 8), :])
        yb_down.start()

    def cols_across():
        yb_up.wait_recv()
        yb_down.wait_recv()
        mid = y * CB
        fill(acc_c, 0, CB, lambda r: m0[at(mid + r, 8), :] + (ry[0, at(r, 8), :] + ry[1, at(r, 8), :]))
        cz.start()

    def cols_final():
        cz.wait_recv()
        fill(cw, col_at(0), CB, lambda r: acc_c[at(r, 8), :] + rcz[at(r, 8), :])
        for copy in cy + cc[:1]:
            copy.start()

    @pl.when(i != j)
    def _():
        scatter[0].wait_recv()

    def piece(k):
        return at((k % 4) * 8, 8)

    firsts = [copies(chunk.at[piece(zh + d)], got.at[d - 1], zs[d - 1]) for d in (1, 2, 3)]
    part = jnp.where(own_row, chunk[piece(zh), :], 0.0)
    for d in (1, 2, 3):
        firsts[d - 1].wait_recv()
        part = part + jnp.where(row_of(zh - d + 4, x) == p, got[d - 1], 0.0)
    mine[...] = part
    seconds = [copies(mine, zgot.at[d - 1], xs[d - 1]) for d in (1, 2, 3)]
    for d in (1, 2, 3):
        seconds[d - 1].wait_recv()
        part = part + zgot[d - 1]
    packed[j, piece(zh), :] = part
    thirds = [copies(packed.at[j, piece(zh)], packed.at[j, piece(zh)], zs[d - 1]) for d in (1, 2, 3)]
    rows_near()
    for copy in thirds:
        copy.wait_recv()
    gather_cols(copies, packed, packed, PR, rows_z_far)

    stages = [
        (rows_z_near, cols_far),
        (cols_near,),
        (rows_final, cols_across),
        (lambda: handed(gx[0], gy[0]), cols_final),
        (lambda: handed(ga, gb + gx[1] + gx[2]), lambda: handed(cy, cy2 + [cc[3], cc[1]])),
        (lambda: handed(gb, gx[3]), lambda: handed(cy2, [cc[2]])),
        (lambda: handed(gx[1] + gx[2], gy[1] + gy[2]),),
        (lambda: handed(gx[3], gy[3]),),
    ]

    for g in range(4):
        for r, start in ((g, 0), (7 - g, 128 * (g + 1))):
            for q in range(r + 1):
                lanes = pl.ds(start + 128 * q, 128)
                tile = jnp.concatenate([packed[4 * g + m, :, lanes] for m in range(4)], axis=0)
                a[pl.ds(128 * r, 128), pl.ds(128 * q, 128)] = tile
                if q < r:
                    a[pl.ds(128 * q, 128), pl.ds(128 * r, 128)] = tile.T
    eye = (lax.broadcasted_iota(jnp.int32, (NB, NB), 0) == lax.broadcasted_iota(jnp.int32, (NB, NB), 1)).astype(f32)

    put(piv, pivot_inverse([a[8 * w : 8 * w + 8, 0:NB] for w in range(NB // 8)]))

    def step(kb, _):
        for n, stage in enumerate(stages[:-1]):

            @pl.when(kb == n)
            def _():
                for part in stage:
                    part()

        sweep(a, piv, us, eye, kb, False)
        return 0

    lax.fori_loop(0, PW // NB - 1, step, 0)
    for part in stages[-1]:
        part()
    sweep(a, piv, us, eye, PW // NB - 1, True)
    outs = [
        pltpu.make_async_copy(cw, cw_out, local.at[0]),
        pltpu.make_async_copy(a, inv_out, local.at[1]),
        pltpu.make_async_copy(rows, rows_out, local.at[2]),
    ]
    handed(cc, [])
    outs[0].start()
    outs[1].start()
    lead = dot3(cw[pl.ds(PW, 64), :], a[...])
    for pair in gy:
        handed(pair, [])
    outs[2].start()

    for t in range(4):
        lanes = pl.ds(256 * t, 256)
        value = hw[pl.ds(PW, 64), lanes] - dot3(lead, rows[:, lanes])
        pruned_ref[:, lanes] = value
        low_ref[:, lanes] = value.astype(bf16)

    copies.drain()
    for copy in outs:
        copy.wait()

    @pl.when(i == j)
    def _():
        for copy in scatter:
            copy.wait_send()


def put(piv, inv):
    for w in range(NB // 8):
        piv[8 * w : 8 * w + 8, :] = inv[w]


def sweep(a, piv, us, eye, kb, last):
    n = PW
    here = pl.ds(pl.multiple_of(kb * NB, NB), NB)
    a[here, here] = eye
    u = dot3(piv[...], a[here, :])
    uh, ul = split(u)
    if not last:
        us[...] = u
        after = pl.ds(pl.multiple_of(kb * NB + NB, NB), NB)
        block = a[after, after] - dot3(a[after, here], us[:, after])
    a[here, here] = -eye
    ch, cl = split(a[:, here])
    a[here, :] = jnp.zeros((NB, n), f32)
    a[:, here] = jnp.zeros((n, NB), f32)
    uk = jnp.concatenate([uh, ul, uh], axis=0)
    ck = jnp.concatenate([ch, ch, cl], axis=1)
    if not last:
        inv = pivot_inverse([block[8 * w : 8 * w + 8, :] for w in range(NB // 8)])
    for t in range(n // 256):
        r = slice(256 * t, 256 * t + 256)
        a[r, :] = a[r, :] - dot(ck[r, :], uk)
    if not last:
        put(piv, inv)


def front(panels, inverse, weight):
    sems = 9 + 25 + 28 + 14
    dma = pltpu.SemaphoreType.DMA

    def buf(*shape):
        return pltpu.VMEM((*shape, PW), f32)

    def out(*shape):
        return jax.ShapeDtypeStruct(shape, f32)

    return pl.pallas_call(
        front_kernel,
        out_shape=(out(PW, PW), out(PW, PW), out(8 * CB, PW), out(64, PW), jax.ShapeDtypeStruct((64, PW), bf16)),
        in_specs=[pl.BlockSpec(memory_space=pltpu.SMEM)] + [pl.BlockSpec(memory_space=pl.ANY)] * 2,
        out_specs=(pl.BlockSpec(memory_space=pl.ANY),) * 3 + (VMEM,) * 2,
        scratch_shapes=[
            buf(PW), buf(PW), buf(8 * CB), buf(NB), buf(8 * CB),
            pltpu.VMEM((16 * PR, PC), f32),
            pltpu.VMEM((PR, PC), f32),
            pltpu.VMEM((3, 8, PC), f32),
            pltpu.VMEM((8, PC), f32),
            pltpu.VMEM((3, 8, PC), f32),
            pltpu.VMEM((16, PR, PC), f32),
            pltpu.VMEM((NB, NB), f32),
            buf(2, 128), buf(2, 256), buf(2, 256), buf(256), buf(2, 32), buf(2, 64), buf(2, 64),
            buf(4 * CB), buf(4 * CB), buf(CT), buf(CB - CT), buf(2, CB), buf(2, CB), buf(CB), buf(CB),
            dma((11,)), dma((15,)), dma, dma((sems,)), dma((sems,)),
        ],
        compiler_params=pltpu.CompilerParams(collective_id=0, has_side_effects=True, vmem_limit_bytes=60 << 20),
        cost_estimate=pl.CostEstimate(flops=60 * 10**9, bytes_accessed=400 * 10**6, transcendentals=0),
        name="front",
    )(panels, inverse, weight)


def gather_cols(copies, first, out, rows, between):
    i, j, zh, x, y, zl, c = place()
    h = rows // 2
    ups, downs, cores = [], [], []
    across = copies(first.at[j], out.at[j], (i, col_of(y, zl + 1, c)))
    up, down = (i, col_of(y + 1, zl, c)), (i, col_of(y + 3, zl, c))
    peer = (i, col_of(y, zl, c + 1))
    for t in (0, 1):
        src = first if t == 0 else out
        if t == 1:
            across.wait_recv()
        s = col_of(y, zl + t, c)
        ups.append(copies(src.at[s], out.at[s], up))
        downs.append(copies(src.at[s], out.at[s], down))
        cores.append(copies(src.at[s], out.at[s], peer))
    halves = []
    for t in (0, 1):
        ups[t].wait_recv()
        s = col_of(y + 3, zl + t, c)
        halves.append(copies(out.at[s, pl.ds(0, h)], out.at[s, pl.ds(0, h)], up))
        cores.append(copies(out.at[s], out.at[s], peer))
        downs[t].wait_recv()
        s = col_of(y + 1, zl + t, c)
        halves.append(copies(out.at[s, pl.ds(h, h)], out.at[s, pl.ds(h, h)], down))
        cores.append(copies(out.at[s], out.at[s], peer))
    between()
    for t in (0, 1):
        halves[2 * t].wait_recv()
        halves[2 * t + 1].wait_recv()
        s = col_of(y + 2, zl + t, c)
        cores.append(copies(out.at[s], out.at[s], peer))
    for copy in cores:
        copy.wait_recv()


def split(x):
    hi = x.astype(bf16)
    return hi, (x - hi.astype(f32)).astype(bf16)


def dot(a, b):
    return jnp.dot(a, b, preferred_element_type=f32)


def dot3(a, b):
    ah, al = split(a)
    bh, bl = split(b)
    return dot(ah, bh) + (dot(ah, bl) + dot(al, bh))


def pivot_inverse(rows):
    full = (8, NB)
    lane = lax.broadcasted_iota(jnp.int32, full, 1)
    sub = lax.broadcasted_iota(jnp.int32, full, 0)
    rows = list(rows)

    def spread(k):
        return [[jnp.broadcast_to(r[:, q : q + 1], full) for r in rows] for q in (k, k + 1)]

    c0, c1 = spread(0)
    for k in range(0, NB, 2):
        v, s = k // 8, k % 8

        def row(x, t):
            return jnp.broadcast_to(x[s + t : s + t + 1, :], full)

        r0, r1 = row(rows[v], 0), row(rows[v], 1)
        p00, p01, p10, p11 = row(c0[v], 0), row(c1[v], 0), row(c0[v], 1), row(c1[v], 1)
        scale = 1.0 / (p00 * p11 - p01 * p10)
        h00, h01, h10, h11 = p11 * scale, -(p01 * scale), -(p10 * scale), p00 * scale
        ahead = spread(k + 2) if k + 2 < NB else ()
        e0, e1 = lane == k, lane == k + 1
        r0 = jnp.where(e0, 1.0, jnp.where(e1, 0.0, r0))
        r1 = jnp.where(e1, 1.0, jnp.where(e0, 0.0, r1))
        u0 = h00 * r0 + h01 * r1
        u1 = h10 * r0 + h11 * r1
        new = []
        for d in ahead:
            b0, b1 = row(d[v], 0), row(d[v], 1)
            g0, g1 = h00 * b0 + h01 * b1, h10 * b0 + h11 * b1
            n = [d[w] - c0[w] * g0 - c1[w] * g1 for w in range(NB // 8)]
            n[v] = jnp.where(sub == s, g0, jnp.where(sub == s + 1, g1, n[v]))
            new.append(n)
        for w in range(NB // 8):
            base = jnp.where(e0 | e1, 0.0, rows[w]) - c0[w] * u0 - c1[w] * u1
            if w == v:
                base = jnp.where(sub == s, u0, jnp.where(sub == s + 1, u1, base))
            rows[w] = base
        if new:
            c0, c1 = new
    return rows


def refresh_kernel(
    scale, low_ref, tok_ref, tgt_ref, inv_ref, rows_ref, cw_ref, res_ref, cor_ref, prod_ref,
    wide_a, wide_b, row_hi, row_lo, sol_hi, sol_lo, local, every, part, heard, own_low, lows,
    s_far, r_far_up, r_far_down, s_up, s_down, r_up, r_down, own,
    z_far, zr_far_up, zr_far_down, z_up, z_down, zr_up, zr_down,
    send, recv, rs_send, rs_recv, ag_send, ag_recv,
):
    i, j, zh, x, y, zl, c = place()
    x_up, x_down = (row_of(zh, x + 1), j), (row_of(zh, x + 3), j)
    z_next, z_prev = (row_of(zh + 1, x), j), (row_of(zh + 3, x), j)
    fetch = [
        pltpu.make_async_copy(rows_ref, wide_a, local.at[0]),
        pltpu.make_async_copy(inv_ref, wide_b, local.at[1]),
        pltpu.make_async_copy(cw_ref.at[pl.ds(0, PW)], wide_a, local.at[2]),
    ]
    fetch[0].start()
    fetch[1].start()
    meet([(i, (j + d) % 16) for d in range(1, 16)] + [x_up, x_down, z_next, z_prev])
    copies = Copies(send, recv)
    tokens = tok_ref[...]
    half = low_ref.shape[0] // 2
    top, bottom = pl.ds(0, half), pl.ds(half, half)

    def rows_split():
        fetch[0].wait()
        for t in range(4):
            r = pl.ds(256 * t, 256)
            row_hi[r, :], row_lo[r, :] = split(wide_a[r, :])
        fetch[2].start()
        fetch[1].wait()

    def solve(t):
        r = pl.ds(256 * t, 256)
        bh, bl = split(wide_b[r, :])
        value = dot(bh, row_hi[...]) + (dot(bh, row_lo[...]) + dot(bl, row_hi[...]))
        sol_hi[r, :], sol_lo[r, :] = split(value)

    def remove(t):
        if t == 0:
            fetch[2].wait()
        r = pl.ds(256 * t, 256)
        ch, cl = split(wide_a[r, :])
        prod_ref[r, :] = dot(ch, sol_hi[...]) + (dot(ch, sol_lo[...]) + dot(cl, sol_hi[...]))

    partials = []

    def use(s, block):
        value = lax.dot_general(block[...], tokens, (((1,), (1,)), ((), ())), preferred_element_type=f32)
        part[s] = value
        copy = pltpu.make_async_remote_copy(
            src_ref=part.at[s],
            dst_ref=heard.at[j],
            send_sem=rs_send.at[s],
            recv_sem=rs_recv.at[j],
            device_id=(i, s),
            device_id_type=MESH,
        )
        pl.when(s != j)(copy.start)
        partials.append((s, copy))

    def spread(s, block):
        return s, copies(block, every.at[s], x_up), copies(block, every.at[s], x_down)

    zn = copies(low_ref, every.at[i], z_next)
    zp = copies(low_ref, every.at[i], z_prev)
    sent = [spread(i, low_ref)]
    use(i, low_ref)
    rows_split()
    solve(0)
    zn.wait_recv()
    s = row_of(zh + 3, x)
    z1 = copies(every.at[s, top], every.at[s, top], z_next)
    sent.append(spread(s, every.at[s]))
    zp.wait_recv()
    s = row_of(zh + 1, x)
    z2 = copies(every.at[s, bottom], every.at[s, bottom], z_prev)
    sent.append(spread(s, every.at[s]))
    use(row_of(zh + 3, x), every.at[row_of(zh + 3, x)])
    use(s, every.at[s])
    solve(1)
    z1.wait_recv()
    z2.wait_recv()
    s = row_of(zh + 2, x)
    sent.append(spread(s, every.at[s]))
    use(s, every.at[s])
    lasts = []
    solve(2)
    for dz, (_, up, down) in zip((0, 3, 1, 2), sent):
        up.wait_recv()
        s = row_of(zh + dz, x + 3)
        a = copies(every.at[s, top], every.at[s, top], x_up)
        use(s, every.at[s])
        down.wait_recv()
        s = row_of(zh + dz, x + 1)
        b = copies(every.at[s, bottom], every.at[s, bottom], x_down)
        use(s, every.at[s])
        lasts.append((dz, a, b))
    solve(3)
    for dz, a, b in lasts:
        a.wait_recv()
        b.wait_recv()
        s = row_of(zh + dz, x + 2)
        use(s, every.at[s])

    remove(0)

    total = part[j] - tgt_ref[...]
    for d in range(1, 16):
        k = (j + d) % 16
        pltpu.make_async_remote_copy(
            src_ref=part.at[k],
            dst_ref=heard.at[k],
            send_sem=rs_send.at[k],
            recv_sem=rs_recv.at[k],
            device_id=(i, k),
            device_id_type=MESH,
        ).wait_recv()
        total = total + heard[k]
    res_ref[...] = total
    own_low[...] = total.astype(bf16)

    shared = []
    for d in range(1, 16):
        copy = pltpu.make_async_remote_copy(
            src_ref=own_low,
            dst_ref=lows.at[j],
            send_sem=ag_send.at[d - 1],
            recv_sem=ag_recv.at[j],
            device_id=(i, (j + d) % 16),
            device_id_type=MESH,
        )
        copy.start()
        shared.append(copy)
    lows[j] = total.astype(bf16)
    remove(1)
    for d in range(1, 16):
        k = (j + d) % 16
        pltpu.make_async_remote_copy(
            src_ref=own_low,
            dst_ref=lows.at[k],
            send_sem=ag_send.at[d - 1],
            recv_sem=ag_recv.at[k],
            device_id=(i, k),
            device_id_type=MESH,
        ).wait_recv()

    def product(zz, xx):
        return dot(lows[row_of(zz, xx)], tokens)

    order = (2, 1, 3, 0)
    far = []
    for q, dz in enumerate(order):
        s_far[q] = product(zh + dz, x + 2).astype(bf16)
        far.append((
            copies(s_far.at[q, top], r_far_up.at[q], x_up),
            copies(s_far.at[q, bottom], r_far_down.at[q], x_down),
        ))
    remove(2)
    near = []
    for q, dz in enumerate(order):
        value = product(zh + dz, x + 1)
        far[q][0].wait_recv()
        s_up[q, top] = (value[:half] + r_far_up[q].astype(f32)).astype(bf16)
        s_up[q, bottom] = value[half:].astype(bf16)
        a = copies(s_up.at[q], r_up.at[q], x_up)
        value = product(zh + dz, x + 3)
        far[q][1].wait_recv()
        s_down[q, top] = value[:half].astype(bf16)
        s_down[q, bottom] = (value[half:] + r_far_down[q].astype(f32)).astype(bf16)
        b = copies(s_down.at[q], r_down.at[q], x_down)
        near.append((a, b))
        own[q] = product(zh + dz, x)

    remove(3)

    def joined(q):
        near[q][0].wait_recv()
        near[q][1].wait_recv()
        return own[q] + (r_up[q].astype(f32) + r_down[q].astype(f32))

    z_far[...] = joined(0).astype(bf16)
    za = copies(z_far.at[top], zr_far_up, z_next)
    zb = copies(z_far.at[bottom], zr_far_down, z_prev)
    value = joined(1)
    z_up[bottom] = value[half:].astype(bf16)
    za.wait_recv()
    z_up[top] = (value[:half] + zr_far_up[...].astype(f32)).astype(bf16)
    zc = copies(z_up, zr_up, z_next)
    value = joined(2)
    z_down[top] = value[:half].astype(bf16)
    zb.wait_recv()
    z_down[bottom] = (value[half:] + zr_far_down[...].astype(f32)).astype(bf16)
    zd = copies(z_down, zr_down, z_prev)
    value = joined(3)
    zc.wait_recv()
    zd.wait_recv()
    cor_ref[...] = (value + (zr_up[...].astype(f32) + zr_down[...].astype(f32))) * scale

    copies.drain()
    for s, copy in partials:
        pl.when(s != j)(copy.wait_send)
    for copy in shared:
        copy.wait_send()


def refresh(low, tokens, targets_t, block_inverse, rows, columns, scale):
    m, n = low.shape
    t = tokens.shape[0]
    sems = 4 + 16 + 16 + 4
    dma = pltpu.SemaphoreType.DMA

    def wide(*lead):
        return pltpu.VMEM((*lead, n), bf16)

    return pl.pallas_call(
        functools.partial(refresh_kernel, scale),
        out_shape=tuple(jax.ShapeDtypeStruct(shape, f32) for shape in ((m, t), (m, n), (n, n))),
        in_specs=[VMEM] * 3 + [pl.BlockSpec(memory_space=pl.ANY)] * 3,
        out_specs=(VMEM,) * 3,
        scratch_shapes=[
            pltpu.VMEM((n, n), f32), pltpu.VMEM((n, n), f32), wide(n), wide(n), wide(n), wide(n), dma((3,)),
            wide(16, m), pltpu.VMEM((16, m, t), f32), pltpu.VMEM((16, m, t), f32),
            pltpu.VMEM((m, t), bf16), pltpu.VMEM((16, m, t), bf16),
            wide(4, m), wide(4, m // 2), wide(4, m // 2), wide(4, m), wide(4, m), wide(4, m), wide(4, m),
            pltpu.VMEM((4, m, n), f32),
            wide(m), wide(m // 2), wide(m // 2), wide(m), wide(m), wide(m), wide(m),
            dma((sems,)), dma((sems,)), dma((16,)), dma((16,)), dma((15,)), dma((16,)),
        ],
        compiler_params=pltpu.CompilerParams(collective_id=1, has_side_effects=True, vmem_limit_bytes=52 << 20),
        cost_estimate=pl.CostEstimate(flops=10**9, bytes_accessed=200 * 10**6, transcendentals=0),
        name="refresh",
    )(low, tokens, targets_t, block_inverse, rows, columns)


def shards(panels, inverse, weight, tokens, targets):
    block_inverse, row_panel, columns, pruned, low = front(panels, inverse, weight)
    token_count = tokens.shape[0] * lax.axis_size("row")
    residual_t, correlation, update = refresh(
        low, tokens, targets.T.astype(f32), block_inverse, row_panel, columns, 1.0 / math.sqrt(token_count)
    )
    return (inverse - update, pruned, residual_t.T, correlation)


def solution(mesh):
    in_specs = (P(), P("row", "col"), P("row", "col"), P("row", "col"), P("row", "col"))
    out_specs = (P("row", "col"), P("row", "col"), P("row", "col"), P("row", "col"))
    return jax.shard_map(shards, mesh=mesh, in_specs=in_specs, out_specs=out_specs, check_vma=False)
```

```python
import functools
import math

import jax
import jax.numpy as jnp
from jax import lax
from jax.experimental import pallas as pl
from jax.experimental.pallas import tpu as pltpu
from jax.sharding import PartitionSpec as P

PW = 1024
NB = 128
MESH = pl.DeviceIdType.MESH
VMEM = pl.BlockSpec(memory_space=pltpu.VMEM)
f32 = jnp.float32
bf16 = jnp.bfloat16


def place():
    i, j = lax.axis_index("row"), lax.axis_index("col")
    return i, j, i // 4, i % 4, j // 4, (j // 2) % 2, j % 2


def row_of(zh, x):
    return (zh % 4) * 4 + x % 4


def col_of(y, zl, c):
    return ((y % 4) * 2 + zl % 2) * 2 + c % 2


class Copies:
    def __init__(self, send, recv):
        self.send, self.recv, self.made = send, recv, []

    def plan(self, src, dst, device):
        n = len(self.made)
        copy = pltpu.make_async_remote_copy(
            src_ref=src,
            dst_ref=dst,
            send_sem=self.send.at[n],
            recv_sem=self.recv.at[n],
            device_id=device,
            device_id_type=MESH,
        )
        self.made.append(copy)
        return copy

    def __call__(self, src, dst, device):
        copy = self.plan(src, dst, device)
        copy.start()
        return copy

    def drain(self):
        for copy in self.made:
            copy.wait_send()


def meet(devices):
    barrier = pltpu.get_barrier_semaphore()
    for device in devices:
        pl.semaphore_signal(barrier, inc=1, device_id=device, device_id_type=MESH)
    pl.semaphore_wait(barrier, len(devices))


PR, PC = 32, 1152
CB = 136
CT = 72


def at(start, size):
    return pl.ds(pl.multiple_of(start, 8), size)


def fill(dst, start, rows, value):
    @pl.loop(0, rows // 8)
    def _(t):
        r = pl.multiple_of(t * 8, 8)
        dst[at(start + r, 8), :] = value(r)


def front_kernel(
    p_ref, h_ref, w_ref, inv_out, rows_out, cw_out, pruned_ref, low_ref,
    a, rows, cw, us, hw, pack, chunk, got, mine, zgot, packed, piv,
    ra, sb, rb, acc, rz, sz, rzn,
    rc, m0, ryu, ryd, sy, ry, acc_c, rcz,
    local, send1, recv1, send, recv,
):
    i, j, zh, x, y, zl, c = place()
    p = p_ref[0]
    loads = [
        pltpu.make_async_copy(h_ref, hw.at[pl.ds(0, PW)], local.at[9]),
        pltpu.make_async_copy(w_ref, hw.at[pl.ds(PW, 64)], local.at[10]),
    ]
    for load in loads:
        load.start()
    xs = [(row_of(zh, x + d), j) for d in (1, 2, 3)]
    zs = [(row_of(zh + d, x), j) for d in (1, 2, 3)]
    meet([(i, (j + d) % 16) for d in range(1, 16)] + xs + zs)
    x_up, x_down, z_next, z_prev = xs[0], xs[2], zs[0], zs[2]
    y_up, y_down = (i, col_of(y + 1, zl, c)), (i, col_of(y + 3, zl, c))
    across, peer = (i, col_of(y, zl + 1, c)), (i, col_of(y, zl, c + 1))
    copies = Copies(send, recv)

    scatter = [
        pltpu.make_async_remote_copy(
            src_ref=pack.at[at(((j + d) % 16) * PR, PR)],
            dst_ref=chunk,
            send_sem=send1.at[d - 1],
            recv_sem=recv1,
            device_id=(i, (j + d) % 16),
            device_id_type=MESH,
        )
        for d in range(1, 16)
    ]

    @pl.when(i == j)
    def _():
        loads = []
        for g in range(4):
            r = pl.ds(128 * g, 128)
            m, n = 128 * (g + 1), 128 * (8 - g)
            loads.append(pltpu.make_async_copy(h_ref.at[r, pl.ds(0, m)], pack.at[r, pl.ds(0, m)], local.at[2 * g]))
            far = pl.ds(128 * (7 - g), 128)
            loads.append(pltpu.make_async_copy(h_ref.at[far, pl.ds(0, n)], pack.at[r, pl.ds(m, n)], local.at[2 * g + 1]))
        for load in loads:
            load.start()
        for load in loads:
            load.wait()
        for copy in scatter:
            copy.start()
        own = pltpu.make_async_copy(pack.at[at(j * PR, PR)], chunk, local.at[8])
        own.start()
        own.wait()

    for load in loads:
        load.wait()

    own_row = i == p
    far = ((x + 2) % 4) * 256
    ra_up = copies(hw.at[at(far, 128)], ra.at[0], x_up)
    ra_down = copies(hw.at[at(far + 128, 128)], ra.at[1], x_down)
    low_half, high_half = pl.ds(0, 128), pl.ds(128, 128)
    rb_up = [copies.plan(sb.at[0, part], rb.at[0, part], x_up) for part in (high_half, low_half)]
    rb_down = [copies.plan(sb.at[1, part], rb.at[1, part], x_down) for part in (low_half, high_half)]
    far = ((zh + 2) % 4) * 64
    za_up = copies.plan(acc.at[at(far, 32)], rz.at[0], z_next)
    za_down = copies.plan(acc.at[at(far + 32, 32)], rz.at[1], z_prev)
    zb_up = copies.plan(sz.at[0], rzn.at[0], z_next)
    zb_down = copies.plan(sz.at[1], rzn.at[1], z_prev)

    def chunk_at(k):
        return x * 256 + ((zh + k) % 4) * 64

    def block_at(k):
        return ((x + k) % 4) * 256

    def same(ref, start, size, device):
        return copies.plan(ref.at[at(start, size)], ref.at[at(start, size)], device)

    ga = [same(rows, chunk_at(0), 64, z_next), same(rows, chunk_at(0), 64, z_prev)]
    gb = [same(rows, chunk_at(3), 32, z_next), same(rows, chunk_at(1) + 32, 32, z_prev)]

    def far_chunk(k, n):
        return ((x + n) % 4) * 256 + ((zh + k) % 4) * 64

    gx = [[same(rows, chunk_at(k), 64, x_up), same(rows, chunk_at(k), 64, x_down)] for k in (0, 1, 3, 2)]
    gy = [
        [same(rows, far_chunk(k, 3), 32, x_up), same(rows, far_chunk(k, 1) + 32, 32, x_down)] for k in (0, 1, 3, 2)
    ]

    def held(r):
        return jnp.where(own_row, hw[at(r, 8), :], 0.0)

    up, down = block_at(1), block_at(3)
    fill(sb.at[0], 128, 128, lambda r: held(up + 128 + r))
    rb_up[0].start()
    fill(sb.at[1], 0, 128, lambda r: held(down + r))
    rb_down[0].start()

    def rows_near():
        before = row_of(zh, x + 3) == p
        after = row_of(zh, x + 1) == p
        ra_up.wait_recv()
        fill(sb.at[0], 0, 128, lambda r: held(up + r) + jnp.where(before, ra[0, at(r, 8), :], 0.0))
        rb_up[1].start()
        ra_down.wait_recv()
        fill(sb.at[1], 128, 128, lambda r: held(down + 128 + r) + jnp.where(after, ra[1, at(r, 8), :], 0.0))
        rb_down[1].start()

    def rows_z_far():
        handed(rb_up + rb_down, [])
        fill(acc, 0, 256, lambda r: held(block_at(0) + r) + (rb[0, at(r, 8), :] + rb[1, at(r, 8), :]))
        za_up.start()
        za_down.start()

    def rows_z_near():
        za_up.wait_recv()
        za_down.wait_recv()
        up, down = ((zh + 1) % 4) * 64, ((zh + 3) % 4) * 64
        fill(sz.at[0], 0, 32, lambda r: acc[at(up + r, 8), :] + rz[0, at(r, 8), :])
        fill(sz.at[0], 32, 32, lambda r: acc[at(up + 32 + r, 8), :])
        zb_up.start()
        fill(sz.at[1], 0, 32, lambda r: acc[at(down + r, 8), :])
        fill(sz.at[1], 32, 32, lambda r: acc[at(down + 32 + r, 8), :] + rz[1, at(r, 8), :])
        zb_down.start()

    def rows_final():
        zb_up.wait_recv()
        zb_down.wait_recv()
        mid = zh * 64
        fill(rows, chunk_at(0), 64, lambda r: acc[at(mid + r, 8), :] + (rzn[0, at(r, 8), :] + rzn[1, at(r, 8), :]))
        for copy in ga + gx[0]:
            copy.start()

    def handed(waits, starts):
        for copy in waits:
            copy.wait_recv()
        for copy in starts:
            copy.start()

    ca = copies(hw.at[at((1 - c) * 4 * CB, 4 * CB)], rc, peer)
    far = ((y + 2) % 4) * CB
    ya_up = copies.plan(m0.at[at(far, CT)], ryu, y_up)
    ya_down = copies.plan(m0.at[at(far + CT, CB - CT)], ryd, y_down)
    yb_up = copies.plan(sy.at[0], ry.at[0], y_up)
    yb_down = copies.plan(sy.at[1], ry.at[1], y_down)
    cz = copies.plan(acc_c, rcz, across)

    def col_at(k):
        return c * 4 * CB + ((y + k) % 4) * CB

    cy = [same(cw, col_at(0), CB, y_up), same(cw, col_at(0), CB, y_down)]
    cy2 = [same(cw, col_at(3), CT, y_up), same(cw, col_at(1) + CT, CB - CT, y_down)]
    cc = [same(cw, col_at(k), CB, peer) for k in range(4)]

    def cols_far():
        ca.wait_recv()
        own, other = j == p, col_of(y, zl, c + 1) == p
        base = c * 4 * CB
        fill(m0, 0, 4 * CB, lambda r: jnp.where(own, hw[at(base + r, 8), :], 0.0) + jnp.where(other, rc[at(r, 8), :], 0.0))
        ya_up.start()
        ya_down.start()

    def cols_near():
        ya_up.wait_recv()
        ya_down.wait_recv()
        up, down = ((y + 1) % 4) * CB, ((y + 3) % 4) * CB
        fill(sy.at[0], 0, CT, lambda r: m0[at(up + r, 8), :] + ryu[at(r, 8), :])
        fill(sy.at[0], CT, CB - CT, lambda r: m0[at(up + CT + r, 8), :])
        yb_up.start()
        fill(sy.at[1], 0, CT, lambda r: m0[at(down + r, 8), :])
        fill(sy.at[1], CT, CB - CT, lambda r: m0[at(down + CT + r, 8), :] + ryd[at(r, 8), :])
        yb_down.start()

    def cols_across():
        yb_up.wait_recv()
        yb_down.wait_recv()
        mid = y * CB
        fill(acc_c, 0, CB, lambda r: m0[at(mid + r, 8), :] + (ry[0, at(r, 8), :] + ry[1, at(r, 8), :]))
        cz.start()

    def cols_final():
        cz.wait_recv()
        fill(cw, col_at(0), CB, lambda r: acc_c[at(r, 8), :] + rcz[at(r, 8), :])
        for copy in cy + cc[:1]:
            copy.start()

    @pl.when(i != j)
    def _():
        scatter[0].wait_recv()

    def piece(k):
        return at((k % 4) * 8, 8)

    firsts = [copies(chunk.at[piece(zh + d)], got.at[d - 1], zs[d - 1]) for d in (1, 2, 3)]
    cols_far()
    part = jnp.where(own_row, chunk[piece(zh), :], 0.0)
    for d in (1, 2, 3):
        firsts[d - 1].wait_recv()
        part = part + jnp.where(row_of(zh - d + 4, x) == p, got[d - 1], 0.0)
    mine[...] = part
    seconds = [copies(mine, zgot.at[d - 1], xs[d - 1]) for d in (1, 2, 3)]
    rows_near()
    for d in (1, 2, 3):
        seconds[d - 1].wait_recv()
        part = part + zgot[d - 1]
    packed[j, piece(zh), :] = part
    thirds = [copies(packed.at[j, piece(zh)], packed.at[j, piece(zh)], zs[d - 1]) for d in (1, 2, 3)]
    cols_near()
    for copy in thirds:
        copy.wait_recv()
    gather_cols(copies, packed, packed, PR, cols_across, rows_z_far)
    rows_z_near()

    stages = [
        (cols_final,),
        (rows_final,),
        (lambda: handed(cy, cy2 + [cc[3], cc[1]]),),
        (lambda: handed(ga, gb + gx[1] + gx[2]), lambda: handed(gx[0], gy[0])),
        (lambda: handed(gb, gx[3]), lambda: handed(cy2, [cc[2]])),
        (lambda: handed(gx[1] + gx[2], gy[1] + gy[2]),),
        (lambda: handed(gx[3], gy[3]),),
        (),
    ]

    for g in range(4):
        for r, start in ((g, 0), (7 - g, 128 * (g + 1))):
            for q in range(r + 1):
                lanes = pl.ds(start + 128 * q, 128)
                tile = jnp.concatenate([packed[4 * g + m, :, lanes] for m in range(4)], axis=0)
                a[pl.ds(128 * r, 128), pl.ds(128 * q, 128)] = tile
                if q < r:
                    a[pl.ds(128 * q, 128), pl.ds(128 * r, 128)] = tile.T
    eye = (lax.broadcasted_iota(jnp.int32, (NB, NB), 0) == lax.broadcasted_iota(jnp.int32, (NB, NB), 1)).astype(f32)

    put(piv, pivot_inverse([a[8 * w : 8 * w + 8, 0:NB] for w in range(NB // 8)]))

    def step(kb, _):
        for n, stage in enumerate(stages[:-1]):

            @pl.when(kb == n)
            def _():
                for part in stage:
                    part()

        sweep(a, piv, us, eye, kb, False)
        return 0

    lax.fori_loop(0, PW // NB - 1, step, 0)
    for part in stages[-1]:
        part()
    sweep(a, piv, us, eye, PW // NB - 1, True)
    outs = [
        pltpu.make_async_copy(cw, cw_out, local.at[0]),
        pltpu.make_async_copy(a, inv_out, local.at[1]),
        pltpu.make_async_copy(rows, rows_out, local.at[2]),
    ]
    handed(cc, [])
    outs[0].start()
    outs[1].start()
    lead = dot3(cw[pl.ds(PW, 64), :], a[...])
    for pair in gy:
        handed(pair, [])
    outs[2].start()

    for t in range(4):
        lanes = pl.ds(256 * t, 256)
        value = hw[pl.ds(PW, 64), lanes] - dot3(lead, rows[:, lanes])
        pruned_ref[:, lanes] = value
        low_ref[:, lanes] = value.astype(bf16)

    copies.drain()
    for copy in outs:
        copy.wait()

    @pl.when(i == j)
    def _():
        for copy in scatter:
            copy.wait_send()


def put(piv, inv):
    for w in range(NB // 8):
        piv[8 * w : 8 * w + 8, :] = inv[w]


def sweep(a, piv, us, eye, kb, last):
    n = PW
    here = pl.ds(pl.multiple_of(kb * NB, NB), NB)
    a[here, here] = eye
    u = dot3(piv[...], a[here, :])
    uh, ul = split(u)
    if not last:
        us[...] = u
        after = pl.ds(pl.multiple_of(kb * NB + NB, NB), NB)
        block = a[after, after] - dot3(a[after, here], us[:, after])
    a[here, here] = -eye
    ch, cl = split(a[:, here])
    a[here, :] = jnp.zeros((NB, n), f32)
    a[:, here] = jnp.zeros((n, NB), f32)
    uk = jnp.concatenate([uh, ul, uh], axis=0)
    ck = jnp.concatenate([ch, ch, cl], axis=1)
    if not last:
        inv = pivot_inverse([block[8 * w : 8 * w + 8, :] for w in range(NB // 8)])
    for t in range(n // 256):
        r = slice(256 * t, 256 * t + 256)
        a[r, :] = a[r, :] - dot(ck[r, :], uk)
    if not last:
        put(piv, inv)


def front(panels, inverse, weight):
    sems = 9 + 25 + 30 + 14
    dma = pltpu.SemaphoreType.DMA

    def buf(*shape):
        return pltpu.VMEM((*shape, PW), f32)

    def out(*shape):
        return jax.ShapeDtypeStruct(shape, f32)

    return pl.pallas_call(
        front_kernel,
        out_shape=(out(PW, PW), out(PW, PW), out(8 * CB, PW), out(64, PW), jax.ShapeDtypeStruct((64, PW), bf16)),
        in_specs=[pl.BlockSpec(memory_space=pltpu.SMEM)] + [pl.BlockSpec(memory_space=pl.ANY)] * 2,
        out_specs=(pl.BlockSpec(memory_space=pl.ANY),) * 3 + (VMEM,) * 2,
        scratch_shapes=[
            buf(PW), buf(PW), buf(8 * CB), buf(NB), buf(8 * CB),
            pltpu.VMEM((16 * PR, PC), f32),
            pltpu.VMEM((PR, PC), f32),
            pltpu.VMEM((3, 8, PC), f32),
            pltpu.VMEM((8, PC), f32),
            pltpu.VMEM((3, 8, PC), f32),
            pltpu.VMEM((16, PR, PC), f32),
            pltpu.VMEM((NB, NB), f32),
            buf(2, 128), buf(2, 256), buf(2, 256), buf(256), buf(2, 32), buf(2, 64), buf(2, 64),
            buf(4 * CB), buf(4 * CB), buf(CT), buf(CB - CT), buf(2, CB), buf(2, CB), buf(CB), buf(CB),
            dma((11,)), dma((15,)), dma, dma((sems,)), dma((sems,)),
        ],
        compiler_params=pltpu.CompilerParams(collective_id=0, has_side_effects=True, vmem_limit_bytes=60 << 20),
        cost_estimate=pl.CostEstimate(flops=60 * 10**9, bytes_accessed=400 * 10**6, transcendentals=0),
        name="front",
    )(panels, inverse, weight)


def gather_cols(copies, first, out, rows, early, between):
    i, j, zh, x, y, zl, c = place()
    h = rows // 2
    ups, downs, cores = [], [], []
    across = copies(first.at[j], out.at[j], (i, col_of(y, zl + 1, c)))
    up, down = (i, col_of(y + 1, zl, c)), (i, col_of(y + 3, zl, c))
    peer = (i, col_of(y, zl, c + 1))
    for t in (0, 1):
        src = first if t == 0 else out
        if t == 1:
            early()
            across.wait_recv()
        s = col_of(y, zl + t, c)
        ups.append(copies(src.at[s], out.at[s], up))
        downs.append(copies(src.at[s], out.at[s], down))
        cores.append(copies(src.at[s], out.at[s], peer))
    halves = []
    for t in (0, 1):
        ups[t].wait_recv()
        s = col_of(y + 3, zl + t, c)
        halves.append(copies(out.at[s, pl.ds(0, h)], out.at[s, pl.ds(0, h)], up))
        cores.append(copies(out.at[s], out.at[s], peer))
        downs[t].wait_recv()
        s = col_of(y + 1, zl + t, c)
        halves.append(copies(out.at[s, pl.ds(h, h)], out.at[s, pl.ds(h, h)], down))
        cores.append(copies(out.at[s], out.at[s], peer))
    between()
    for t in (0, 1):
        halves[2 * t].wait_recv()
        halves[2 * t + 1].wait_recv()
        s = col_of(y + 2, zl + t, c)
        cores.append(copies(out.at[s], out.at[s], peer))
    for copy in cores:
        copy.wait_recv()


def split(x):
    hi = x.astype(bf16)
    return hi, (x - hi.astype(f32)).astype(bf16)


def dot(a, b):
    return jnp.dot(a, b, preferred_element_type=f32)


def dot3(a, b):
    ah, al = split(a)
    bh, bl = split(b)
    return dot(ah, bh) + (dot(ah, bl) + dot(al, bh))


def pivot_inverse(rows):
    full = (8, NB)
    lane = lax.broadcasted_iota(jnp.int32, full, 1)
    sub = lax.broadcasted_iota(jnp.int32, full, 0)
    rows = list(rows)

    def spread(k):
        return [[jnp.broadcast_to(r[:, q : q + 1], full) for r in rows] for q in (k, k + 1)]

    c0, c1 = spread(0)
    for k in range(0, NB, 2):
        v, s = k // 8, k % 8

        def row(x, t):
            return jnp.broadcast_to(x[s + t : s + t + 1, :], full)

        r0, r1 = row(rows[v], 0), row(rows[v], 1)
        p00, p01, p10, p11 = row(c0[v], 0), row(c1[v], 0), row(c0[v], 1), row(c1[v], 1)
        scale = 1.0 / (p00 * p11 - p01 * p10)
        h00, h01, h10, h11 = p11 * scale, -(p01 * scale), -(p10 * scale), p00 * scale
        ahead = spread(k + 2) if k + 2 < NB else ()
        e0, e1 = lane == k, lane == k + 1
        r0 = jnp.where(e0, 1.0, jnp.where(e1, 0.0, r0))
        r1 = jnp.where(e1, 1.0, jnp.where(e0, 0.0, r1))
        u0 = h00 * r0 + h01 * r1
        u1 = h10 * r0 + h11 * r1
        new = []
        for d in ahead:
            b0, b1 = row(d[v], 0), row(d[v], 1)
            g0, g1 = h00 * b0 + h01 * b1, h10 * b0 + h11 * b1
            n = [d[w] - c0[w] * g0 - c1[w] * g1 for w in range(NB // 8)]
            n[v] = jnp.where(sub == s, g0, jnp.where(sub == s + 1, g1, n[v]))
            new.append(n)
        for w in range(NB // 8):
            base = jnp.where(e0 | e1, 0.0, rows[w]) - c0[w] * u0 - c1[w] * u1
            if w == v:
                base = jnp.where(sub == s, u0, jnp.where(sub == s + 1, u1, base))
            rows[w] = base
        if new:
            c0, c1 = new
    return rows


def refresh_kernel(
    scale, low_ref, tok_ref, tgt_ref, inv_ref, rows_ref, cw_ref, res_ref, cor_ref, prod_ref,
    wide_a, wide_b, row_hi, row_lo, sol_hi, sol_lo, local, every, part, heard, own_low, lows,
    s_far, r_far_up, r_far_down, s_up, s_down, r_up, r_down, own,
    z_far, zr_far_up, zr_far_down, z_up, z_down, zr_up, zr_down,
    send, recv, rs_send, rs_recv, ag_send, ag_recv,
):
    i, j, zh, x, y, zl, c = place()
    x_up, x_down = (row_of(zh, x + 1), j), (row_of(zh, x + 3), j)
    z_next, z_prev = (row_of(zh + 1, x), j), (row_of(zh + 3, x), j)
    fetch = [
        pltpu.make_async_copy(rows_ref, wide_a, local.at[0]),
        pltpu.make_async_copy(inv_ref, wide_b, local.at[1]),
        pltpu.make_async_copy(cw_ref.at[pl.ds(0, PW)], wide_a, local.at[2]),
    ]
    fetch[0].start()
    fetch[1].start()
    meet([(i, (j + d) % 16) for d in range(1, 16)] + [x_up, x_down, z_next, z_prev])
    copies = Copies(send, recv)
    tokens = tok_ref[...]
    half = low_ref.shape[0] // 2
    top, bottom = pl.ds(0, half), pl.ds(half, half)

    def rows_split():
        fetch[0].wait()
        for t in range(4):
            r = pl.ds(256 * t, 256)
            row_hi[r, :], row_lo[r, :] = split(wide_a[r, :])
        fetch[2].start()
        fetch[1].wait()

    def solve(t):
        r = pl.ds(256 * t, 256)
        bh, bl = split(wide_b[r, :])
        value = dot(bh, row_hi[...]) + (dot(bh, row_lo[...]) + dot(bl, row_hi[...]))
        sol_hi[r, :], sol_lo[r, :] = split(value)

    def remove(t):
        if t == 0:
            fetch[2].wait()
        r = pl.ds(256 * t, 256)
        ch, cl = split(wide_a[r, :])
        prod_ref[r, :] = dot(ch, sol_hi[...]) + (dot(ch, sol_lo[...]) + dot(cl, sol_hi[...]))

    partials = []

    def use(s, block):
        value = lax.dot_general(block[...], tokens, (((1,), (1,)), ((), ())), preferred_element_type=f32)
        part[s] = value
        copy = pltpu.make_async_remote_copy(
            src_ref=part.at[s],
            dst_ref=heard.at[j],
            send_sem=rs_send.at[s],
            recv_sem=rs_recv.at[j],
            device_id=(i, s),
            device_id_type=MESH,
        )
        pl.when(s != j)(copy.start)
        partials.append((s, copy))

    def spread(s, block):
        return s, copies(block, every.at[s], x_up), copies(block, every.at[s], x_down)

    zn = copies(low_ref, every.at[i], z_next)
    zp = copies(low_ref, every.at[i], z_prev)
    sent = [spread(i, low_ref)]
    use(i, low_ref)
    rows_split()
    solve(0)
    zn.wait_recv()
    s = row_of(zh + 3, x)
    z1 = copies(every.at[s, top], every.at[s, top], z_next)
    sent.append(spread(s, every.at[s]))
    zp.wait_recv()
    s = row_of(zh + 1, x)
    z2 = copies(every.at[s, bottom], every.at[s, bottom], z_prev)
    sent.append(spread(s, every.at[s]))
    use(row_of(zh + 3, x), every.at[row_of(zh + 3, x)])
    use(s, every.at[s])
    solve(1)
    z1.wait_recv()
    z2.wait_recv()
    s = row_of(zh + 2, x)
    sent.append(spread(s, every.at[s]))
    use(s, every.at[s])
    lasts = []
    solve(2)
    for dz, (_, up, down) in zip((0, 3, 1, 2), sent):
        up.wait_recv()
        s = row_of(zh + dz, x + 3)
        a = copies(every.at[s, top], every.at[s, top], x_up)
        use(s, every.at[s])
        down.wait_recv()
        s = row_of(zh + dz, x + 1)
        b = copies(every.at[s, bottom], every.at[s, bottom], x_down)
        use(s, every.at[s])
        lasts.append((dz, a, b))
    solve(3)
    for dz, a, b in lasts:
        a.wait_recv()
        b.wait_recv()
        s = row_of(zh + dz, x + 2)
        use(s, every.at[s])

    remove(0)

    total = part[j] - tgt_ref[...]
    for d in range(1, 16):
        k = (j + d) % 16
        pltpu.make_async_remote_copy(
            src_ref=part.at[k],
            dst_ref=heard.at[k],
            send_sem=rs_send.at[k],
            recv_sem=rs_recv.at[k],
            device_id=(i, k),
            device_id_type=MESH,
        ).wait_recv()
        total = total + heard[k]
    res_ref[...] = total
    own_low[...] = total.astype(bf16)

    shared = []
    for d in range(1, 16):
        copy = pltpu.make_async_remote_copy(
            src_ref=own_low,
            dst_ref=lows.at[j],
            send_sem=ag_send.at[d - 1],
            recv_sem=ag_recv.at[j],
            device_id=(i, (j + d) % 16),
            device_id_type=MESH,
        )
        copy.start()
        shared.append(copy)
    lows[j] = total.astype(bf16)
    remove(1)
    for d in range(1, 16):
        k = (j + d) % 16
        pltpu.make_async_remote_copy(
            src_ref=own_low,
            dst_ref=lows.at[k],
            send_sem=ag_send.at[d - 1],
            recv_sem=ag_recv.at[k],
            device_id=(i, k),
            device_id_type=MESH,
        ).wait_recv()

    def product(zz, xx):
        return dot(lows[row_of(zz, xx)], tokens)

    order = (2, 1, 3, 0)
    far = []
    for q, dz in enumerate(order):
        s_far[q] = product(zh + dz, x + 2).astype(bf16)
        far.append((
            copies(s_far.at[q, top], r_far_up.at[q], x_up),
            copies(s_far.at[q, bottom], r_far_down.at[q], x_down),
        ))
    remove(2)
    near = []
    for q, dz in enumerate(order):
        value = product(zh + dz, x + 1)
        far[q][0].wait_recv()
        s_up[q, top] = (value[:half] + r_far_up[q].astype(f32)).astype(bf16)
        s_up[q, bottom] = value[half:].astype(bf16)
        a = copies(s_up.at[q], r_up.at[q], x_up)
        value = product(zh + dz, x + 3)
        far[q][1].wait_recv()
        s_down[q, top] = value[:half].astype(bf16)
        s_down[q, bottom] = (value[half:] + r_far_down[q].astype(f32)).astype(bf16)
        b = copies(s_down.at[q], r_down.at[q], x_down)
        near.append((a, b))
        own[q] = product(zh + dz, x)

    remove(3)

    def joined(q):
        near[q][0].wait_recv()
        near[q][1].wait_recv()
        return own[q] + (r_up[q].astype(f32) + r_down[q].astype(f32))

    z_far[...] = joined(0).astype(bf16)
    za = copies(z_far.at[top], zr_far_up, z_next)
    zb = copies(z_far.at[bottom], zr_far_down, z_prev)
    value = joined(1)
    z_up[bottom] = value[half:].astype(bf16)
    za.wait_recv()
    z_up[top] = (value[:half] + zr_far_up[...].astype(f32)).astype(bf16)
    zc = copies(z_up, zr_up, z_next)
    value = joined(2)
    z_down[top] = value[:half].astype(bf16)
    zb.wait_recv()
    z_down[bottom] = (value[half:] + zr_far_down[...].astype(f32)).astype(bf16)
    zd = copies(z_down, zr_down, z_prev)
    value = joined(3)
    zc.wait_recv()
    zd.wait_recv()
    cor_ref[...] = (value + (zr_up[...].astype(f32) + zr_down[...].astype(f32))) * scale

    copies.drain()
    for s, copy in partials:
        pl.when(s != j)(copy.wait_send)
    for copy in shared:
        copy.wait_send()


def refresh(low, tokens, targets_t, block_inverse, rows, columns, scale):
    m, n = low.shape
    t = tokens.shape[0]
    sems = 4 + 16 + 16 + 4
    dma = pltpu.SemaphoreType.DMA

    def wide(*lead):
        return pltpu.VMEM((*lead, n), bf16)

    return pl.pallas_call(
        functools.partial(refresh_kernel, scale),
        out_shape=tuple(jax.ShapeDtypeStruct(shape, f32) for shape in ((m, t), (m, n), (n, n))),
        in_specs=[VMEM] * 3 + [pl.BlockSpec(memory_space=pl.ANY)] * 3,
        out_specs=(VMEM,) * 3,
        scratch_shapes=[
            pltpu.VMEM((n, n), f32), pltpu.VMEM((n, n), f32), wide(n), wide(n), wide(n), wide(n), dma((3,)),
            wide(16, m), pltpu.VMEM((16, m, t), f32), pltpu.VMEM((16, m, t), f32),
            pltpu.VMEM((m, t), bf16), pltpu.VMEM((16, m, t), bf16),
            wide(4, m), wide(4, m // 2), wide(4, m // 2), wide(4, m), wide(4, m), wide(4, m), wide(4, m),
            pltpu.VMEM((4, m, n), f32),
            wide(m), wide(m // 2), wide(m // 2), wide(m), wide(m), wide(m), wide(m),
            dma((sems,)), dma((sems,)), dma((16,)), dma((16,)), dma((15,)), dma((16,)),
        ],
        compiler_params=pltpu.CompilerParams(collective_id=1, has_side_effects=True, vmem_limit_bytes=52 << 20),
        cost_estimate=pl.CostEstimate(flops=10**9, bytes_accessed=200 * 10**6, transcendentals=0),
        name="refresh",
    )(low, tokens, targets_t, block_inverse, rows, columns)


def shards(panels, inverse, weight, tokens, targets):
    block_inverse, row_panel, columns, pruned, low = front(panels, inverse, weight)
    token_count = tokens.shape[0] * lax.axis_size("row")
    residual_t, correlation, update = refresh(
        low, tokens, targets.T.astype(f32), block_inverse, row_panel, columns, 1.0 / math.sqrt(token_count)
    )
    return (inverse - update, pruned, residual_t.T, correlation)


def solution(mesh):
    in_specs = (P(), P("row", "col"), P("row", "col"), P("row", "col"), P("row", "col"))
    out_specs = (P("row", "col"), P("row", "col"), P("row", "col"), P("row", "col"))
    return jax.shard_map(shards, mesh=mesh, in_specs=in_specs, out_specs=out_specs, check_vma=False)
```

```python
import functools
import math

import jax
import jax.numpy as jnp
from jax import lax
from jax.experimental import pallas as pl
from jax.experimental.pallas import tpu as pltpu
from jax.sharding import PartitionSpec as P

PW = 1024
NB = 128
MESH = pl.DeviceIdType.MESH
VMEM = pl.BlockSpec(memory_space=pltpu.VMEM)
f32 = jnp.float32
bf16 = jnp.bfloat16


def place():
    i, j = lax.axis_index("row"), lax.axis_index("col")
    return i, j, i // 4, i % 4, j // 4, (j // 2) % 2, j % 2


def row_of(zh, x):
    return (zh % 4) * 4 + x % 4


def col_of(y, zl, c):
    return ((y % 4) * 2 + zl % 2) * 2 + c % 2


class Copies:
    def __init__(self, send, recv):
        self.send, self.recv, self.made = send, recv, []

    def plan(self, src, dst, device):
        n = len(self.made)
        copy = pltpu.make_async_remote_copy(
            src_ref=src,
            dst_ref=dst,
            send_sem=self.send.at[n],
            recv_sem=self.recv.at[n],
            device_id=device,
            device_id_type=MESH,
        )
        self.made.append(copy)
        return copy

    def __call__(self, src, dst, device):
        copy = self.plan(src, dst, device)
        copy.start()
        return copy

    def drain(self):
        for copy in self.made:
            copy.wait_send()


def meet(devices):
    barrier = pltpu.get_barrier_semaphore()
    for device in devices:
        pl.semaphore_signal(barrier, inc=1, device_id=device, device_id_type=MESH)
    pl.semaphore_wait(barrier, len(devices))


PR, PC = 32, 1152
CB = 136
CT = 72


def at(start, size):
    return pl.ds(pl.multiple_of(start, 8), size)


def fill(dst, start, rows, value):
    if rows <= CB:
        dst[at(start, rows), :] = value(0, rows)
        return

    @pl.loop(0, rows // 32)
    def _(t):
        r = pl.multiple_of(t * 32, 32)
        dst[at(start + r, 32), :] = value(r, 32)


def front_kernel(
    p_ref, h_ref, w_ref, inv_out, rows_out, cw_out, pruned_ref, low_ref,
    a, rows, cw, us, hw, pack, chunk, got, mine, zgot, packed, piv,
    ra, sb, rb, acc, rz, sz, rzn,
    rc, m0, ryu, ryd, sy, ry, acc_c, rcz,
    local, send1, recv1, send, recv,
):
    i, j, zh, x, y, zl, c = place()
    p = p_ref[0]
    loads = [
        pltpu.make_async_copy(h_ref, hw.at[pl.ds(0, PW)], local.at[9]),
        pltpu.make_async_copy(w_ref, hw.at[pl.ds(PW, 64)], local.at[10]),
    ]
    for load in loads:
        load.start()
    xs = [(row_of(zh, x + d), j) for d in (1, 2, 3)]
    zs = [(row_of(zh + d, x), j) for d in (1, 2, 3)]
    meet([(i, (j + d) % 16) for d in range(1, 16)] + xs + zs)
    x_up, x_down, z_next, z_prev = xs[0], xs[2], zs[0], zs[2]
    y_up, y_down = (i, col_of(y + 1, zl, c)), (i, col_of(y + 3, zl, c))
    across, peer = (i, col_of(y, zl + 1, c)), (i, col_of(y, zl, c + 1))
    copies = Copies(send, recv)

    scatter = [
        pltpu.make_async_remote_copy(
            src_ref=pack.at[at(((j + d) % 16) * PR, PR)],
            dst_ref=chunk,
            send_sem=send1.at[d - 1],
            recv_sem=recv1,
            device_id=(i, (j + d) % 16),
            device_id_type=MESH,
        )
        for d in range(1, 16)
    ]

    @pl.when(i == j)
    def _():
        loads = []
        for g in range(4):
            r = pl.ds(128 * g, 128)
            m, n = 128 * (g + 1), 128 * (8 - g)
            loads.append(pltpu.make_async_copy(h_ref.at[r, pl.ds(0, m)], pack.at[r, pl.ds(0, m)], local.at[2 * g]))
            far = pl.ds(128 * (7 - g), 128)
            loads.append(pltpu.make_async_copy(h_ref.at[far, pl.ds(0, n)], pack.at[r, pl.ds(m, n)], local.at[2 * g + 1]))
        for load in loads:
            load.start()
        for load in loads:
            load.wait()
        for copy in scatter:
            copy.start()
        own = pltpu.make_async_copy(pack.at[at(j * PR, PR)], chunk, local.at[8])
        own.start()
        own.wait()

    for load in loads:
        load.wait()

    own_row = i == p
    far = ((x + 2) % 4) * 256
    ra_up = copies(hw.at[at(far, 128)], ra.at[0], x_up)
    ra_down = copies(hw.at[at(far + 128, 128)], ra.at[1], x_down)
    low_half, high_half = pl.ds(0, 128), pl.ds(128, 128)
    rb_up = [copies.plan(sb.at[0, part], rb.at[0, part], x_up) for part in (high_half, low_half)]
    rb_down = [copies.plan(sb.at[1, part], rb.at[1, part], x_down) for part in (low_half, high_half)]
    far = ((zh + 2) % 4) * 64
    za_up = copies.plan(acc.at[at(far, 32)], rz.at[0], z_next)
    za_down = copies.plan(acc.at[at(far + 32, 32)], rz.at[1], z_prev)
    zb_up = copies.plan(sz.at[0], rzn.at[0], z_next)
    zb_down = copies.plan(sz.at[1], rzn.at[1], z_prev)

    def chunk_at(k):
        return x * 256 + ((zh + k) % 4) * 64

    def block_at(k):
        return ((x + k) % 4) * 256

    def same(ref, start, size, device):
        return copies.plan(ref.at[at(start, size)], ref.at[at(start, size)], device)

    ga = [same(rows, chunk_at(0), 64, z_next), same(rows, chunk_at(0), 64, z_prev)]
    gb = [same(rows, chunk_at(3), 32, z_next), same(rows, chunk_at(1) + 32, 32, z_prev)]

    def far_chunk(k, n):
        return ((x + n) % 4) * 256 + ((zh + k) % 4) * 64

    gx = [[same(rows, chunk_at(k), 64, x_up), same(rows, chunk_at(k), 64, x_down)] for k in (0, 1, 3, 2)]
    gy = [
        [same(rows, far_chunk(k, 3), 32, x_up), same(rows, far_chunk(k, 1) + 32, 32, x_down)] for k in (0, 1, 3, 2)
    ]

    def held(r, n):
        return jnp.where(own_row, hw[at(r, n), :], 0.0)

    up, down = block_at(1), block_at(3)
    fill(sb.at[0], 128, 128, lambda r, n: held(up + 128 + r, n))
    rb_up[0].start()
    fill(sb.at[1], 0, 128, lambda r, n: held(down + r, n))
    rb_down[0].start()

    def rows_near():
        before = row_of(zh, x + 3) == p
        after = row_of(zh, x + 1) == p
        ra_up.wait_recv()
        fill(sb.at[0], 0, 128, lambda r, n: held(up + r, n) + jnp.where(before, ra[0, at(r, n), :], 0.0))
        rb_up[1].start()
        ra_down.wait_recv()
        fill(sb.at[1], 128, 128, lambda r, n: held(down + 128 + r, n) + jnp.where(after, ra[1, at(r, n), :], 0.0))
        rb_down[1].start()

    def rows_z_far():
        handed(rb_up + rb_down, [])
        fill(acc, 0, 256, lambda r, n: held(block_at(0) + r, n) + (rb[0, at(r, n), :] + rb[1, at(r, n), :]))
        za_up.start()
        za_down.start()

    def rows_z_near():
        za_up.wait_recv()
        za_down.wait_recv()
        up, down = ((zh + 1) % 4) * 64, ((zh + 3) % 4) * 64
        fill(sz.at[0], 0, 32, lambda r, n: acc[at(up + r, n), :] + rz[0, at(r, n), :])
        fill(sz.at[0], 32, 32, lambda r, n: acc[at(up + 32 + r, n), :])
        zb_up.start()
        fill(sz.at[1], 0, 32, lambda r, n: acc[at(down + r, n), :])
        fill(sz.at[1], 32, 32, lambda r, n: acc[at(down + 32 + r, n), :] + rz[1, at(r, n), :])
        zb_down.start()

    def rows_final():
        zb_up.wait_recv()
        zb_down.wait_recv()
        mid = zh * 64
        fill(rows, chunk_at(0), 64, lambda r, n: acc[at(mid + r, n), :] + (rzn[0, at(r, n), :] + rzn[1, at(r, n), :]))
        for copy in ga + gx[0]:
            copy.start()

    def handed(waits, starts):
        for copy in waits:
            copy.wait_recv()
        for copy in starts:
            copy.start()

    ca = copies(hw.at[at((1 - c) * 4 * CB, 4 * CB)], rc, peer)
    far = ((y + 2) % 4) * CB
    ya_up = copies.plan(m0.at[at(far, CT)], ryu, y_up)
    ya_down = copies.plan(m0.at[at(far + CT, CB - CT)], ryd, y_down)
    yb_up = copies.plan(sy.at[0], ry.at[0], y_up)
    yb_down = copies.plan(sy.at[1], ry.at[1], y_down)
    cz = copies.plan(acc_c, rcz, across)

    def col_at(k):
        return c * 4 * CB + ((y + k) % 4) * CB

    cy = [same(cw, col_at(0), CB, y_up), same(cw, col_at(0), CB, y_down)]
    cy2 = [same(cw, col_at(3), CT, y_up), same(cw, col_at(1) + CT, CB - CT, y_down)]
    cc = [same(cw, col_at(k), CB, peer) for k in range(4)]

    def cols_far():
        ca.wait_recv()
        own, other = j == p, col_of(y, zl, c + 1) == p
        base = c * 4 * CB
        fill(m0, 0, 4 * CB, lambda r, n: jnp.where(own, hw[at(base + r, n), :], 0.0) + jnp.where(other, rc[at(r, n), :], 0.0))
        ya_up.start()
        ya_down.start()

    def cols_near():
        ya_up.wait_recv()
        ya_down.wait_recv()
        up, down = ((y + 1) % 4) * CB, ((y + 3) % 4) * CB
        fill(sy.at[0], 0, CT, lambda r, n: m0[at(up + r, n), :] + ryu[at(r, n), :])
        fill(sy.at[0], CT, CB - CT, lambda r, n: m0[at(up + CT + r, n), :])
        yb_up.start()
        fill(sy.at[1], 0, CT, lambda r, n: m0[at(down + r, n), :])
        fill(sy.at[1], CT, CB - CT, lambda r, n: m0[at(down + CT + r, n), :] + ryd[at(r, n), :])
        yb_down.start()

    def cols_across():
        yb_up.wait_recv()
        yb_down.wait_recv()
        mid = y * CB
        fill(acc_c, 0, CB, lambda r, n: m0[at(mid + r, n), :] + (ry[0, at(r, n), :] + ry[1, at(r, n), :]))
        cz.start()

    def cols_final():
        cz.wait_recv()
        fill(cw, col_at(0), CB, lambda r, n: acc_c[at(r, n), :] + rcz[at(r, n), :])
        for copy in cy + cc[:1]:
            copy.start()

    @pl.when(i != j)
    def _():
        scatter[0].wait_recv()

    def piece(k):
        return at((k % 4) * 8, 8)

    firsts = [copies(chunk.at[piece(zh + d)], got.at[d - 1], zs[d - 1]) for d in (1, 2, 3)]
    cols_far()
    part = jnp.where(own_row, chunk[piece(zh), :], 0.0)
    for d in (1, 2, 3):
        firsts[d - 1].wait_recv()
        part = part + jnp.where(row_of(zh - d + 4, x) == p, got[d - 1], 0.0)
    mine[...] = part
    seconds = [copies(mine, zgot.at[d - 1], xs[d - 1]) for d in (1, 2, 3)]
    rows_near()
    for d in (1, 2, 3):
        seconds[d - 1].wait_recv()
        part = part + zgot[d - 1]
    packed[j, piece(zh), :] = part
    thirds = [copies(packed.at[j, piece(zh)], packed.at[j, piece(zh)], zs[d - 1]) for d in (1, 2, 3)]
    cols_near()
    for copy in thirds:
        copy.wait_recv()
    gather_cols(copies, packed, packed, PR, cols_across, rows_z_far)
    rows_z_near()

    stages = [
        (cols_final,),
        (rows_final,),
        (lambda: handed(cy, cy2 + [cc[3], cc[1]]),),
        (lambda: handed(ga, gb + gx[1] + gx[2]), lambda: handed(gx[0], gy[0])),
        (lambda: handed(gb, gx[3]), lambda: handed(cy2, [cc[2]])),
        (lambda: handed(gx[1] + gx[2], gy[1] + gy[2]),),
        (lambda: handed(gx[3], gy[3]),),
        (),
    ]

    for g in range(4):
        for r, start in ((g, 0), (7 - g, 128 * (g + 1))):
            for q in range(r + 1):
                lanes = pl.ds(start + 128 * q, 128)
                tile = jnp.concatenate([packed[4 * g + m, :, lanes] for m in range(4)], axis=0)
                a[pl.ds(128 * r, 128), pl.ds(128 * q, 128)] = tile
                if q < r:
                    a[pl.ds(128 * q, 128), pl.ds(128 * r, 128)] = tile.T
    eye = (lax.broadcasted_iota(jnp.int32, (NB, NB), 0) == lax.broadcasted_iota(jnp.int32, (NB, NB), 1)).astype(f32)

    put(piv, pivot_inverse([a[8 * w : 8 * w + 8, 0:NB] for w in range(NB // 8)]))

    def step(kb, _):
        for n, stage in enumerate(stages[:-1]):

            @pl.when(kb == n)
            def _():
                for part in stage:
                    part()

        sweep(a, piv, us, eye, kb, False)
        return 0

    lax.fori_loop(0, PW // NB - 1, step, 0)
    for part in stages[-1]:
        part()
    sweep(a, piv, us, eye, PW // NB - 1, True)
    outs = [
        pltpu.make_async_copy(cw, cw_out, local.at[0]),
        pltpu.make_async_copy(a, inv_out, local.at[1]),
        pltpu.make_async_copy(rows, rows_out, local.at[2]),
    ]
    handed(cc, [])
    outs[0].start()
    outs[1].start()
    lead = dot3_few(cw[pl.ds(PW, 64), :], a[...])
    for pair in gy:
        handed(pair, [])
    outs[2].start()

    for t in range(4):
        lanes = pl.ds(256 * t, 256)
        value = hw[pl.ds(PW, 64), lanes] - dot3_few(lead, rows[:, lanes])
        pruned_ref[:, lanes] = value
        low_ref[:, lanes] = value.astype(bf16)

    copies.drain()
    for copy in outs:
        copy.wait()

    @pl.when(i == j)
    def _():
        for copy in scatter:
            copy.wait_send()


def put(piv, inv):
    for w in range(NB // 8):
        piv[8 * w : 8 * w + 8, :] = inv[w]


def sweep(a, piv, us, eye, kb, last):
    n = PW
    here = pl.ds(pl.multiple_of(kb * NB, NB), NB)
    a[here, here] = eye
    u = dot3(piv[...], a[here, :])
    uh, ul = split(u)
    if not last:
        us[...] = u
        after = pl.ds(pl.multiple_of(kb * NB + NB, NB), NB)
        block = a[after, after] - dot3(a[after, here], us[:, after])
    a[here, here] = -eye
    ch, cl = split(a[:, here])
    a[here, :] = jnp.zeros((NB, n), f32)
    a[:, here] = jnp.zeros((n, NB), f32)
    uk = jnp.concatenate([uh, ul, uh], axis=0)
    ck = jnp.concatenate([ch, ch, cl], axis=1)
    if not last:
        inv = pivot_inverse([block[8 * w : 8 * w + 8, :] for w in range(NB // 8)])
    for t in range(n // 256):
        r = slice(256 * t, 256 * t + 256)
        a[r, :] = a[r, :] - dot(ck[r, :], uk)
    if not last:
        put(piv, inv)


def front(panels, inverse, weight):
    sems = 9 + 25 + 30 + 14
    dma = pltpu.SemaphoreType.DMA

    def buf(*shape):
        return pltpu.VMEM((*shape, PW), f32)

    def out(*shape):
        return jax.ShapeDtypeStruct(shape, f32)

    return pl.pallas_call(
        front_kernel,
        out_shape=(out(PW, PW), out(PW, PW), out(8 * CB, PW), out(64, PW), jax.ShapeDtypeStruct((64, PW), bf16)),
        in_specs=[pl.BlockSpec(memory_space=pltpu.SMEM)] + [pl.BlockSpec(memory_space=pl.ANY)] * 2,
        out_specs=(pl.BlockSpec(memory_space=pl.ANY),) * 3 + (VMEM,) * 2,
        scratch_shapes=[
            buf(PW), buf(PW), buf(8 * CB), buf(NB), buf(8 * CB),
            pltpu.VMEM((16 * PR, PC), f32),
            pltpu.VMEM((PR, PC), f32),
            pltpu.VMEM((3, 8, PC), f32),
            pltpu.VMEM((8, PC), f32),
            pltpu.VMEM((3, 8, PC), f32),
            pltpu.VMEM((16, PR, PC), f32),
            pltpu.VMEM((NB, NB), f32),
            buf(2, 128), buf(2, 256), buf(2, 256), buf(256), buf(2, 32), buf(2, 64), buf(2, 64),
            buf(4 * CB), buf(4 * CB), buf(CT), buf(CB - CT), buf(2, CB), buf(2, CB), buf(CB), buf(CB),
            dma((11,)), dma((15,)), dma, dma((sems,)), dma((sems,)),
        ],
        compiler_params=pltpu.CompilerParams(collective_id=0, has_side_effects=True, vmem_limit_bytes=60 << 20),
        cost_estimate=pl.CostEstimate(flops=60 * 10**9, bytes_accessed=400 * 10**6, transcendentals=0),
        name="front",
    )(panels, inverse, weight)


def gather_cols(copies, first, out, rows, early, between):
    i, j, zh, x, y, zl, c = place()
    h = rows // 2
    ups, downs, cores = [], [], []
    across = copies(first.at[j], out.at[j], (i, col_of(y, zl + 1, c)))
    up, down = (i, col_of(y + 1, zl, c)), (i, col_of(y + 3, zl, c))
    peer = (i, col_of(y, zl, c + 1))
    for t in (0, 1):
        src = first if t == 0 else out
        if t == 1:
            early()
            across.wait_recv()
        s = col_of(y, zl + t, c)
        ups.append(copies(src.at[s], out.at[s], up))
        downs.append(copies(src.at[s], out.at[s], down))
        cores.append(copies(src.at[s], out.at[s], peer))
    halves = []
    for t in (0, 1):
        ups[t].wait_recv()
        s = col_of(y + 3, zl + t, c)
        halves.append(copies(out.at[s, pl.ds(0, h)], out.at[s, pl.ds(0, h)], up))
        cores.append(copies(out.at[s], out.at[s], peer))
        downs[t].wait_recv()
        s = col_of(y + 1, zl + t, c)
        halves.append(copies(out.at[s, pl.ds(h, h)], out.at[s, pl.ds(h, h)], down))
        cores.append(copies(out.at[s], out.at[s], peer))
    between()
    for t in (0, 1):
        halves[2 * t].wait_recv()
        halves[2 * t + 1].wait_recv()
        s = col_of(y + 2, zl + t, c)
        cores.append(copies(out.at[s], out.at[s], peer))
    for copy in cores:
        copy.wait_recv()


def split(x):
    hi = x.astype(bf16)
    return hi, (x - hi.astype(f32)).astype(bf16)


def dot(a, b):
    return jnp.dot(a, b, preferred_element_type=f32)


def dot3(a, b):
    ah, al = split(a)
    bh, bl = split(b)
    return dot(ah, bh) + (dot(ah, bl) + dot(al, bh))


def dot3_few(a, b):
    m = a.shape[0]
    ah, al = split(a)
    bh, bl = split(b)
    both = dot(jnp.concatenate([ah, al], axis=0), bh)
    return both[:m] + (dot(ah, bl) + both[m:])


def pivot_inverse(rows):
    full = (8, NB)
    lane = lax.broadcasted_iota(jnp.int32, full, 1)
    sub = lax.broadcasted_iota(jnp.int32, full, 0)
    rows = list(rows)

    def spread(k):
        return [[jnp.broadcast_to(r[:, q : q + 1], full) for r in rows] for q in (k, k + 1)]

    c0, c1 = spread(0)
    for k in range(0, NB, 2):
        v, s = k // 8, k % 8

        def row(x, t):
            return jnp.broadcast_to(x[s + t : s + t + 1, :], full)

        r0, r1 = row(rows[v], 0), row(rows[v], 1)
        p00, p01, p10, p11 = row(c0[v], 0), row(c1[v], 0), row(c0[v], 1), row(c1[v], 1)
        scale = 1.0 / (p00 * p11 - p01 * p10)
        h00, h01, h10, h11 = p11 * scale, -(p01 * scale), -(p10 * scale), p00 * scale
        ahead = spread(k + 2) if k + 2 < NB else ()
        e0, e1 = lane == k, lane == k + 1
        r0 = jnp.where(e0, 1.0, jnp.where(e1, 0.0, r0))
        r1 = jnp.where(e1, 1.0, jnp.where(e0, 0.0, r1))
        u0 = h00 * r0 + h01 * r1
        u1 = h10 * r0 + h11 * r1
        new = []
        for d in ahead:
            b0, b1 = row(d[v], 0), row(d[v], 1)
            g0, g1 = h00 * b0 + h01 * b1, h10 * b0 + h11 * b1
            n = [d[w] - c0[w] * g0 - c1[w] * g1 for w in range(NB // 8)]
            n[v] = jnp.where(sub == s, g0, jnp.where(sub == s + 1, g1, n[v]))
            new.append(n)
        for w in range(NB // 8):
            base = jnp.where(e0 | e1, 0.0, rows[w]) - c0[w] * u0 - c1[w] * u1
            if w == v:
                base = jnp.where(sub == s, u0, jnp.where(sub == s + 1, u1, base))
            rows[w] = base
        if new:
            c0, c1 = new
    return rows


def refresh_kernel(
    scale, low_ref, tok_ref, tgt_ref, inv_ref, rows_ref, cw_ref, res_ref, cor_ref, prod_ref,
    wide_a, wide_b, row_hi, row_lo, sol_hi, sol_lo, local, every, part, heard, own_low, lows,
    s_far, r_far_up, r_far_down, s_up, s_down, r_up, r_down, own,
    z_far, zr_far_up, zr_far_down, z_up, z_down, zr_up, zr_down,
    send, recv, rs_send, rs_recv, ag_send, ag_recv,
):
    i, j, zh, x, y, zl, c = place()
    x_up, x_down = (row_of(zh, x + 1), j), (row_of(zh, x + 3), j)
    z_next, z_prev = (row_of(zh + 1, x), j), (row_of(zh + 3, x), j)
    fetch = [
        pltpu.make_async_copy(rows_ref, wide_a, local.at[0]),
        pltpu.make_async_copy(inv_ref, wide_b, local.at[1]),
        pltpu.make_async_copy(cw_ref.at[pl.ds(0, PW)], wide_a, local.at[2]),
    ]
    fetch[0].start()
    fetch[1].start()
    meet([(i, (j + d) % 16) for d in range(1, 16)] + [x_up, x_down, z_next, z_prev])
    copies = Copies(send, recv)
    tokens = tok_ref[...]
    half = low_ref.shape[0] // 2
    top, bottom = pl.ds(0, half), pl.ds(half, half)

    def rows_split():
        fetch[0].wait()
        for t in range(4):
            r = pl.ds(256 * t, 256)
            row_hi[r, :], row_lo[r, :] = split(wide_a[r, :])
        fetch[2].start()
        fetch[1].wait()

    def solve(t):
        r = pl.ds(256 * t, 256)
        bh, bl = split(wide_b[r, :])
        value = dot(bh, row_hi[...]) + (dot(bh, row_lo[...]) + dot(bl, row_hi[...]))
        sol_hi[r, :], sol_lo[r, :] = split(value)

    def remove(t):
        if t == 0:
            fetch[2].wait()
        r = pl.ds(256 * t, 256)
        ch, cl = split(wide_a[r, :])
        prod_ref[r, :] = dot(ch, sol_hi[...]) + (dot(ch, sol_lo[...]) + dot(cl, sol_hi[...]))

    partials = []

    def use(s, block):
        value = lax.dot_general(block[...], tokens, (((1,), (1,)), ((), ())), preferred_element_type=f32)
        part[s] = value
        copy = pltpu.make_async_remote_copy(
            src_ref=part.at[s],
            dst_ref=heard.at[j],
            send_sem=rs_send.at[s],
            recv_sem=rs_recv.at[j],
            device_id=(i, s),
            device_id_type=MESH,
        )
        pl.when(s != j)(copy.start)
        partials.append((s, copy))

    def spread(s, block):
        return s, copies(block, every.at[s], x_up), copies(block, every.at[s], x_down)

    zn = copies(low_ref, every.at[i], z_next)
    zp = copies(low_ref, every.at[i], z_prev)
    sent = [spread(i, low_ref)]
    use(i, low_ref)
    zn.wait_recv()
    before = row_of(zh + 3, x)
    z1 = copies(every.at[before, top], every.at[before, top], z_next)
    sent.append(spread(before, every.at[before]))
    zp.wait_recv()
    after = row_of(zh + 1, x)
    z2 = copies(every.at[after, bottom], every.at[after, bottom], z_prev)
    sent.append(spread(after, every.at[after]))
    use(before, every.at[before])
    use(after, every.at[after])
    rows_split()
    z1.wait_recv()
    z2.wait_recv()
    s = row_of(zh + 2, x)
    sent.append(spread(s, every.at[s]))
    use(s, every.at[s])
    lasts = []
    for t, (dz, (_, up, down)) in enumerate(zip((0, 3, 1, 2), sent)):
        up.wait_recv()
        before = row_of(zh + dz, x + 3)
        a = copies(every.at[before, top], every.at[before, top], x_up)
        down.wait_recv()
        after = row_of(zh + dz, x + 1)
        b = copies(every.at[after, bottom], every.at[after, bottom], x_down)
        use(before, every.at[before])
        use(after, every.at[after])
        lasts.append((dz, a, b))
        solve(t)
    for dz, a, b in lasts:
        a.wait_recv()
        b.wait_recv()
        s = row_of(zh + dz, x + 2)
        use(s, every.at[s])

    remove(0)

    total = part[j] - tgt_ref[...]
    for d in range(1, 16):
        k = (j + d) % 16
        pltpu.make_async_remote_copy(
            src_ref=part.at[k],
            dst_ref=heard.at[k],
            send_sem=rs_send.at[k],
            recv_sem=rs_recv.at[k],
            device_id=(i, k),
            device_id_type=MESH,
        ).wait_recv()
        total = total + heard[k]
    res_ref[...] = total
    own_low[...] = total.astype(bf16)

    shared = []
    for d in range(1, 16):
        copy = pltpu.make_async_remote_copy(
            src_ref=own_low,
            dst_ref=lows.at[j],
            send_sem=ag_send.at[d - 1],
            recv_sem=ag_recv.at[j],
            device_id=(i, (j + d) % 16),
            device_id_type=MESH,
        )
        copy.start()
        shared.append(copy)
    lows[j] = total.astype(bf16)
    remove(1)
    for d in range(1, 16):
        k = (j + d) % 16
        pltpu.make_async_remote_copy(
            src_ref=own_low,
            dst_ref=lows.at[k],
            send_sem=ag_send.at[d - 1],
            recv_sem=ag_recv.at[k],
            device_id=(i, k),
            device_id_type=MESH,
        ).wait_recv()

    def product(zz, xx):
        return dot(lows[row_of(zz, xx)], tokens)

    order = (2, 1, 3, 0)
    far = []
    for q, dz in enumerate(order):
        s_far[q] = product(zh + dz, x + 2).astype(bf16)
        far.append((
            copies(s_far.at[q, top], r_far_up.at[q], x_up),
            copies(s_far.at[q, bottom], r_far_down.at[q], x_down),
        ))
    remove(2)
    near = []
    for q, dz in enumerate(order):
        value = product(zh + dz, x + 1)
        far[q][0].wait_recv()
        s_up[q, top] = (value[:half] + r_far_up[q].astype(f32)).astype(bf16)
        s_up[q, bottom] = value[half:].astype(bf16)
        a = copies(s_up.at[q], r_up.at[q], x_up)
        value = product(zh + dz, x + 3)
        far[q][1].wait_recv()
        s_down[q, top] = value[:half].astype(bf16)
        s_down[q, bottom] = (value[half:] + r_far_down[q].astype(f32)).astype(bf16)
        b = copies(s_down.at[q], r_down.at[q], x_down)
        near.append((a, b))
        own[q] = product(zh + dz, x)

    remove(3)

    def joined(q):
        near[q][0].wait_recv()
        near[q][1].wait_recv()
        return own[q] + (r_up[q].astype(f32) + r_down[q].astype(f32))

    z_far[...] = joined(0).astype(bf16)
    za = copies(z_far.at[top], zr_far_up, z_next)
    zb = copies(z_far.at[bottom], zr_far_down, z_prev)
    value = joined(1)
    z_up[bottom] = value[half:].astype(bf16)
    za.wait_recv()
    z_up[top] = (value[:half] + zr_far_up[...].astype(f32)).astype(bf16)
    zc = copies(z_up, zr_up, z_next)
    value = joined(2)
    z_down[top] = value[:half].astype(bf16)
    zb.wait_recv()
    z_down[bottom] = (value[half:] + zr_far_down[...].astype(f32)).astype(bf16)
    zd = copies(z_down, zr_down, z_prev)
    value = joined(3)
    zc.wait_recv()
    zd.wait_recv()
    cor_ref[...] = (value + (zr_up[...].astype(f32) + zr_down[...].astype(f32))) * scale

    copies.drain()
    for s, copy in partials:
        pl.when(s != j)(copy.wait_send)
    for copy in shared:
        copy.wait_send()


def refresh(low, tokens, targets_t, block_inverse, rows, columns, scale):
    m, n = low.shape
    t = tokens.shape[0]
    sems = 4 + 16 + 16 + 4
    dma = pltpu.SemaphoreType.DMA

    def wide(*lead):
        return pltpu.VMEM((*lead, n), bf16)

    return pl.pallas_call(
        functools.partial(refresh_kernel, scale),
        out_shape=tuple(jax.ShapeDtypeStruct(shape, f32) for shape in ((m, t), (m, n), (n, n))),
        in_specs=[VMEM] * 3 + [pl.BlockSpec(memory_space=pl.ANY)] * 3,
        out_specs=(VMEM,) * 3,
        scratch_shapes=[
            pltpu.VMEM((n, n), f32), pltpu.VMEM((n, n), f32), wide(n), wide(n), wide(n), wide(n), dma((3,)),
            wide(16, m), pltpu.VMEM((16, m, t), f32), pltpu.VMEM((16, m, t), f32),
            pltpu.VMEM((m, t), bf16), pltpu.VMEM((16, m, t), bf16),
            wide(4, m), wide(4, m // 2), wide(4, m // 2), wide(4, m), wide(4, m), wide(4, m), wide(4, m),
            pltpu.VMEM((4, m, n), f32),
            wide(m), wide(m // 2), wide(m // 2), wide(m), wide(m), wide(m), wide(m),
            dma((sems,)), dma((sems,)), dma((16,)), dma((16,)), dma((15,)), dma((16,)),
        ],
        compiler_params=pltpu.CompilerParams(collective_id=1, has_side_effects=True, vmem_limit_bytes=52 << 20),
        cost_estimate=pl.CostEstimate(flops=10**9, bytes_accessed=200 * 10**6, transcendentals=0),
        name="refresh",
    )(low, tokens, targets_t, block_inverse, rows, columns)


def shards(panels, inverse, weight, tokens, targets):
    block_inverse, row_panel, columns, pruned, low = front(panels, inverse, weight)
    token_count = tokens.shape[0] * lax.axis_size("row")
    residual_t, correlation, update = refresh(
        low, tokens, targets.T.astype(f32), block_inverse, row_panel, columns, 1.0 / math.sqrt(token_count)
    )
    return (inverse - update, pruned, residual_t.T, correlation)


def solution(mesh):
    in_specs = (P(), P("row", "col"), P("row", "col"), P("row", "col"), P("row", "col"))
    out_specs = (P("row", "col"), P("row", "col"), P("row", "col"), P("row", "col"))
    return jax.shard_map(shards, mesh=mesh, in_specs=in_specs, out_specs=out_specs, check_vma=False)
```

```python
import functools
import math

import jax
import jax.numpy as jnp
from jax import lax
from jax.experimental import pallas as pl
from jax.experimental.pallas import tpu as pltpu
from jax.sharding import PartitionSpec as P

PW = 1024
NB = 128
MESH = pl.DeviceIdType.MESH
VMEM = pl.BlockSpec(memory_space=pltpu.VMEM)
f32 = jnp.float32
bf16 = jnp.bfloat16


def place():
    i, j = lax.axis_index("row"), lax.axis_index("col")
    return i, j, i // 4, i % 4, j // 4, (j // 2) % 2, j % 2


def row_of(zh, x):
    return (zh % 4) * 4 + x % 4


def col_of(y, zl, c):
    return ((y % 4) * 2 + zl % 2) * 2 + c % 2


class Copies:
    def __init__(self, send, recv):
        self.send, self.recv, self.made = send, recv, []

    def plan(self, src, dst, device):
        n = len(self.made)
        copy = pltpu.make_async_remote_copy(
            src_ref=src,
            dst_ref=dst,
            send_sem=self.send.at[n],
            recv_sem=self.recv.at[n],
            device_id=device,
            device_id_type=MESH,
        )
        self.made.append(copy)
        return copy

    def __call__(self, src, dst, device):
        copy = self.plan(src, dst, device)
        copy.start()
        return copy

    def drain(self):
        for copy in self.made:
            copy.wait_send()


def meet(devices):
    barrier = pltpu.get_barrier_semaphore()
    for device in devices:
        pl.semaphore_signal(barrier, inc=1, device_id=device, device_id_type=MESH)
    pl.semaphore_wait(barrier, len(devices))


PR, PC = 32, 1152
CB = 136
CT = 72


def at(start, size):
    return pl.ds(pl.multiple_of(start, 8), size)


def fill(dst, start, rows, value):
    if rows <= CB:
        dst[at(start, rows), :] = value(0, rows)
        return

    @pl.loop(0, rows // 32)
    def _(t):
        r = pl.multiple_of(t * 32, 32)
        dst[at(start + r, 32), :] = value(r, 32)


def front_kernel(
    p_ref, h_ref, w_ref, inv_out, rows_out, cw_out, pruned_ref, low_ref,
    a, rows, cw, us, hw, pack, chunk, got, mine, zgot, packed, piv,
    ra, sb, rb, acc, rz, sz, rzn,
    rc, m0, ryu, ryd, sy, ry, acc_c, rcz,
    local, send1, recv1, send, recv,
):
    i, j, zh, x, y, zl, c = place()
    p = p_ref[0]
    loads = [
        pltpu.make_async_copy(h_ref, hw.at[pl.ds(0, PW)], local.at[9]),
        pltpu.make_async_copy(w_ref, hw.at[pl.ds(PW, 64)], local.at[10]),
    ]
    for load in loads:
        load.start()
    xs = [(row_of(zh, x + d), j) for d in (1, 2, 3)]
    zs = [(row_of(zh + d, x), j) for d in (1, 2, 3)]
    meet([(i, (j + d) % 16) for d in range(1, 16)] + xs + zs)
    x_up, x_down, z_next, z_prev = xs[0], xs[2], zs[0], zs[2]
    y_up, y_down = (i, col_of(y + 1, zl, c)), (i, col_of(y + 3, zl, c))
    across, peer = (i, col_of(y, zl + 1, c)), (i, col_of(y, zl, c + 1))
    copies = Copies(send, recv)

    scatter = [
        pltpu.make_async_remote_copy(
            src_ref=pack.at[at(((j + d) % 16) * PR, PR)],
            dst_ref=chunk,
            send_sem=send1.at[d - 1],
            recv_sem=recv1,
            device_id=(i, (j + d) % 16),
            device_id_type=MESH,
        )
        for d in range(1, 16)
    ]

    @pl.when(i == j)
    def _():
        loads = []
        for g in range(4):
            r = pl.ds(128 * g, 128)
            m, n = 128 * (g + 1), 128 * (8 - g)
            loads.append(pltpu.make_async_copy(h_ref.at[r, pl.ds(0, m)], pack.at[r, pl.ds(0, m)], local.at[2 * g]))
            far = pl.ds(128 * (7 - g), 128)
            loads.append(pltpu.make_async_copy(h_ref.at[far, pl.ds(0, n)], pack.at[r, pl.ds(m, n)], local.at[2 * g + 1]))
        for load in loads:
            load.start()
        for load in loads:
            load.wait()
        for copy in scatter:
            copy.start()
        own = pltpu.make_async_copy(pack.at[at(j * PR, PR)], chunk, local.at[8])
        own.start()
        own.wait()

    for load in loads:
        load.wait()

    own_row = i == p
    far = ((x + 2) % 4) * 256
    ra_up = copies(hw.at[at(far, 128)], ra.at[0], x_up)
    ra_down = copies(hw.at[at(far + 128, 128)], ra.at[1], x_down)
    low_half, high_half = pl.ds(0, 128), pl.ds(128, 128)
    rb_up = [copies.plan(sb.at[0, part], rb.at[0, part], x_up) for part in (high_half, low_half)]
    rb_down = [copies.plan(sb.at[1, part], rb.at[1, part], x_down) for part in (low_half, high_half)]
    far = ((zh + 2) % 4) * 64
    za_up = copies.plan(acc.at[at(far, 32)], rz.at[0], z_next)
    za_down = copies.plan(acc.at[at(far + 32, 32)], rz.at[1], z_prev)
    zb_up = copies.plan(sz.at[0], rzn.at[0], z_next)
    zb_down = copies.plan(sz.at[1], rzn.at[1], z_prev)

    def chunk_at(k):
        return x * 256 + ((zh + k) % 4) * 64

    def block_at(k):
        return ((x + k) % 4) * 256

    def same(ref, start, size, device):
        return copies.plan(ref.at[at(start, size)], ref.at[at(start, size)], device)

    ga = [same(rows, chunk_at(0), 64, z_next), same(rows, chunk_at(0), 64, z_prev)]
    gb = [same(rows, chunk_at(3), 32, z_next), same(rows, chunk_at(1) + 32, 32, z_prev)]

    def far_chunk(k, n):
        return ((x + n) % 4) * 256 + ((zh + k) % 4) * 64

    gx = [[same(rows, chunk_at(k), 64, x_up), same(rows, chunk_at(k), 64, x_down)] for k in (0, 1, 3, 2)]
    gy = [
        [same(rows, far_chunk(k, 3), 32, x_up), same(rows, far_chunk(k, 1) + 32, 32, x_down)] for k in (0, 1, 3, 2)
    ]

    def held(r, n):
        return jnp.where(own_row, hw[at(r, n), :], 0.0)

    up, down = block_at(1), block_at(3)
    fill(sb.at[0], 128, 128, lambda r, n: held(up + 128 + r, n))
    rb_up[0].start()
    fill(sb.at[1], 0, 128, lambda r, n: held(down + r, n))
    rb_down[0].start()

    def rows_near():
        before = row_of(zh, x + 3) == p
        after = row_of(zh, x + 1) == p
        ra_up.wait_recv()
        fill(sb.at[0], 0, 128, lambda r, n: held(up + r, n) + jnp.where(before, ra[0, at(r, n), :], 0.0))
        rb_up[1].start()
        ra_down.wait_recv()
        fill(sb.at[1], 128, 128, lambda r, n: held(down + 128 + r, n) + jnp.where(after, ra[1, at(r, n), :], 0.0))
        rb_down[1].start()

    def rows_z_far():
        handed(rb_up + rb_down, [])
        fill(acc, 0, 256, lambda r, n: held(block_at(0) + r, n) + (rb[0, at(r, n), :] + rb[1, at(r, n), :]))
        za_up.start()
        za_down.start()

    def rows_z_near():
        za_up.wait_recv()
        za_down.wait_recv()
        up, down = ((zh + 1) % 4) * 64, ((zh + 3) % 4) * 64
        fill(sz.at[0], 0, 32, lambda r, n: acc[at(up + r, n), :] + rz[0, at(r, n), :])
        fill(sz.at[0], 32, 32, lambda r, n: acc[at(up + 32 + r, n), :])
        zb_up.start()
        fill(sz.at[1], 0, 32, lambda r, n: acc[at(down + r, n), :])
        fill(sz.at[1], 32, 32, lambda r, n: acc[at(down + 32 + r, n), :] + rz[1, at(r, n), :])
        zb_down.start()

    def rows_final():
        zb_up.wait_recv()
        zb_down.wait_recv()
        mid = zh * 64
        fill(rows, chunk_at(0), 64, lambda r, n: acc[at(mid + r, n), :] + (rzn[0, at(r, n), :] + rzn[1, at(r, n), :]))
        for copy in ga + gx[0]:
            copy.start()

    def handed(waits, starts):
        for copy in waits:
            copy.wait_recv()
        for copy in starts:
            copy.start()

    ca = copies(hw.at[at((1 - c) * 4 * CB, 4 * CB)], rc, peer)
    far = ((y + 2) % 4) * CB
    ya_up = copies.plan(m0.at[at(far, CT)], ryu, y_up)
    ya_down = copies.plan(m0.at[at(far + CT, CB - CT)], ryd, y_down)
    yb_up = copies.plan(sy.at[0], ry.at[0], y_up)
    yb_down = copies.plan(sy.at[1], ry.at[1], y_down)
    cz = copies.plan(acc_c, rcz, across)

    def col_at(k):
        return c * 4 * CB + ((y + k) % 4) * CB

    cy = [same(cw, col_at(0), CB, y_up), same(cw, col_at(0), CB, y_down)]
    cy2 = [same(cw, col_at(3), CT, y_up), same(cw, col_at(1) + CT, CB - CT, y_down)]
    cc = [same(cw, col_at(k), CB, peer) for k in range(4)]

    def cols_far():
        ca.wait_recv()
        own, other = j == p, col_of(y, zl, c + 1) == p
        base = c * 4 * CB
        fill(m0, 0, 4 * CB, lambda r, n: jnp.where(own, hw[at(base + r, n), :], 0.0) + jnp.where(other, rc[at(r, n), :], 0.0))
        ya_up.start()
        ya_down.start()

    def cols_near():
        ya_up.wait_recv()
        ya_down.wait_recv()
        up, down = ((y + 1) % 4) * CB, ((y + 3) % 4) * CB
        fill(sy.at[0], 0, CT, lambda r, n: m0[at(up + r, n), :] + ryu[at(r, n), :])
        fill(sy.at[0], CT, CB - CT, lambda r, n: m0[at(up + CT + r, n), :])
        yb_up.start()
        fill(sy.at[1], 0, CT, lambda r, n: m0[at(down + r, n), :])
        fill(sy.at[1], CT, CB - CT, lambda r, n: m0[at(down + CT + r, n), :] + ryd[at(r, n), :])
        yb_down.start()

    def cols_across():
        yb_up.wait_recv()
        yb_down.wait_recv()
        mid = y * CB
        fill(acc_c, 0, CB, lambda r, n: m0[at(mid + r, n), :] + (ry[0, at(r, n), :] + ry[1, at(r, n), :]))
        cz.start()

    def cols_final():
        cz.wait_recv()
        fill(cw, col_at(0), CB, lambda r, n: acc_c[at(r, n), :] + rcz[at(r, n), :])
        for copy in cy + cc[:1]:
            copy.start()

    @pl.when(i != j)
    def _():
        scatter[0].wait_recv()

    def piece(k):
        return at((k % 4) * 8, 8)

    firsts = [copies(chunk.at[piece(zh + d)], got.at[d - 1], zs[d - 1]) for d in (1, 2, 3)]
    cols_far()
    part = jnp.where(own_row, chunk[piece(zh), :], 0.0)
    for d in (1, 2, 3):
        firsts[d - 1].wait_recv()
        part = part + jnp.where(row_of(zh - d + 4, x) == p, got[d - 1], 0.0)
    mine[...] = part
    seconds = [copies(mine, zgot.at[d - 1], xs[d - 1]) for d in (1, 2, 3)]
    rows_near()
    for d in (1, 2, 3):
        seconds[d - 1].wait_recv()
        part = part + zgot[d - 1]
    packed[j, piece(zh), :] = part
    thirds = [copies(packed.at[j, piece(zh)], packed.at[j, piece(zh)], zs[d - 1]) for d in (1, 2, 3)]
    cols_near()
    for copy in thirds:
        copy.wait_recv()
    gather_cols(copies, packed, packed, PR, cols_across, rows_z_far)

    stages = [
        (rows_z_near, cols_final),
        (),
        (rows_final, lambda: handed(cy, cy2 + [cc[3], cc[1]])),
        (lambda: handed(gx[0], gy[0]),),
        (lambda: handed(ga, gb + gx[1] + gx[2]), lambda: handed(cy2, [cc[2]])),
        (lambda: handed(gb, gx[3]),),
        (lambda: handed(gx[1] + gx[2], gy[1] + gy[2]),),
        (lambda: handed(gx[3], gy[3]),),
    ]

    for g in range(4):
        for r, start in ((g, 0), (7 - g, 128 * (g + 1))):
            for q in range(r + 1):
                lanes = pl.ds(start + 128 * q, 128)
                tile = jnp.concatenate([packed[4 * g + m, :, lanes] for m in range(4)], axis=0)
                a[pl.ds(128 * r, 128), pl.ds(128 * q, 128)] = tile
                if q < r:
                    a[pl.ds(128 * q, 128), pl.ds(128 * r, 128)] = tile.T
    eye = (lax.broadcasted_iota(jnp.int32, (NB, NB), 0) == lax.broadcasted_iota(jnp.int32, (NB, NB), 1)).astype(f32)

    put(piv, pivot_inverse([a[8 * w : 8 * w + 8, 0:NB] for w in range(NB // 8)]))

    def step(kb, _):
        for n, stage in enumerate(stages[:-1]):

            @pl.when(kb == n)
            def _():
                for part in stage:
                    part()

        sweep(a, piv, us, eye, kb, False)
        return 0

    lax.fori_loop(0, PW // NB - 1, step, 0)
    for part in stages[-1]:
        part()
    sweep(a, piv, us, eye, PW // NB - 1, True)
    outs = [
        pltpu.make_async_copy(cw, cw_out, local.at[0]),
        pltpu.make_async_copy(a, inv_out, local.at[1]),
        pltpu.make_async_copy(rows, rows_out, local.at[2]),
    ]
    handed(cc, [])
    outs[0].start()
    outs[1].start()
    lead = dot3_few(cw[pl.ds(PW, 64), :], a[...])
    for pair in gy:
        handed(pair, [])
    outs[2].start()

    for t in range(4):
        lanes = pl.ds(256 * t, 256)
        value = hw[pl.ds(PW, 64), lanes] - dot3_few(lead, rows[:, lanes])
        pruned_ref[:, lanes] = value
        low_ref[:, lanes] = value.astype(bf16)

    copies.drain()
    for copy in outs:
        copy.wait()

    @pl.when(i == j)
    def _():
        for copy in scatter:
            copy.wait_send()


def put(piv, inv):
    for w in range(NB // 8):
        piv[8 * w : 8 * w + 8, :] = inv[w]


def sweep(a, piv, us, eye, kb, last):
    n = PW
    here = pl.ds(pl.multiple_of(kb * NB, NB), NB)
    a[here, here] = eye
    u = dot3(piv[...], a[here, :])
    uh, ul = split(u)
    if not last:
        us[...] = u
        after = pl.ds(pl.multiple_of(kb * NB + NB, NB), NB)
        block = a[after, after] - dot3(a[after, here], us[:, after])
    a[here, here] = -eye
    ch, cl = split(a[:, here])
    a[here, :] = jnp.zeros((NB, n), f32)
    a[:, here] = jnp.zeros((n, NB), f32)
    uk = jnp.concatenate([uh, ul, uh], axis=0)
    ck = jnp.concatenate([ch, ch, cl], axis=1)
    if not last:
        inv = pivot_inverse([block[8 * w : 8 * w + 8, :] for w in range(NB // 8)])
    for t in range(n // 256):
        r = slice(256 * t, 256 * t + 256)
        a[r, :] = a[r, :] - dot(ck[r, :], uk)
    if not last:
        put(piv, inv)


def front(panels, inverse, weight):
    sems = 9 + 25 + 30 + 14
    dma = pltpu.SemaphoreType.DMA

    def buf(*shape):
        return pltpu.VMEM((*shape, PW), f32)

    def out(*shape):
        return jax.ShapeDtypeStruct(shape, f32)

    return pl.pallas_call(
        front_kernel,
        out_shape=(out(PW, PW), out(PW, PW), out(8 * CB, PW), out(64, PW), jax.ShapeDtypeStruct((64, PW), bf16)),
        in_specs=[pl.BlockSpec(memory_space=pltpu.SMEM)] + [pl.BlockSpec(memory_space=pl.ANY)] * 2,
        out_specs=(pl.BlockSpec(memory_space=pl.ANY),) * 3 + (VMEM,) * 2,
        scratch_shapes=[
            buf(PW), buf(PW), buf(8 * CB), buf(NB), buf(8 * CB),
            pltpu.VMEM((16 * PR, PC), f32),
            pltpu.VMEM((PR, PC), f32),
            pltpu.VMEM((3, 8, PC), f32),
            pltpu.VMEM((8, PC), f32),
            pltpu.VMEM((3, 8, PC), f32),
            pltpu.VMEM((16, PR, PC), f32),
            pltpu.VMEM((NB, NB), f32),
            buf(2, 128), buf(2, 256), buf(2, 256), buf(256), buf(2, 32), buf(2, 64), buf(2, 64),
            buf(4 * CB), buf(4 * CB), buf(CT), buf(CB - CT), buf(2, CB), buf(2, CB), buf(CB), buf(CB),
            dma((11,)), dma((15,)), dma, dma((sems,)), dma((sems,)),
        ],
        compiler_params=pltpu.CompilerParams(collective_id=0, has_side_effects=True, vmem_limit_bytes=60 << 20),
        cost_estimate=pl.CostEstimate(flops=60 * 10**9, bytes_accessed=400 * 10**6, transcendentals=0),
        name="front",
    )(panels, inverse, weight)


def gather_cols(copies, first, out, rows, early, between):
    i, j, zh, x, y, zl, c = place()
    h = rows // 2
    ups, downs, cores = [], [], []
    across = copies(first.at[j], out.at[j], (i, col_of(y, zl + 1, c)))
    up, down = (i, col_of(y + 1, zl, c)), (i, col_of(y + 3, zl, c))
    peer = (i, col_of(y, zl, c + 1))
    for t in (0, 1):
        src = first if t == 0 else out
        if t == 1:
            early()
            across.wait_recv()
        s = col_of(y, zl + t, c)
        ups.append(copies(src.at[s], out.at[s], up))
        downs.append(copies(src.at[s], out.at[s], down))
        cores.append(copies(src.at[s], out.at[s], peer))
    halves = []
    for t in (0, 1):
        ups[t].wait_recv()
        s = col_of(y + 3, zl + t, c)
        halves.append(copies(out.at[s, pl.ds(0, h)], out.at[s, pl.ds(0, h)], up))
        cores.append(copies(out.at[s], out.at[s], peer))
        downs[t].wait_recv()
        s = col_of(y + 1, zl + t, c)
        halves.append(copies(out.at[s, pl.ds(h, h)], out.at[s, pl.ds(h, h)], down))
        cores.append(copies(out.at[s], out.at[s], peer))
    between()
    for t in (0, 1):
        halves[2 * t].wait_recv()
        halves[2 * t + 1].wait_recv()
        s = col_of(y + 2, zl + t, c)
        cores.append(copies(out.at[s], out.at[s], peer))
    for copy in cores:
        copy.wait_recv()


def split(x):
    hi = x.astype(bf16)
    return hi, (x - hi.astype(f32)).astype(bf16)


def dot(a, b):
    return jnp.dot(a, b, preferred_element_type=f32)


def dot3(a, b):
    ah, al = split(a)
    bh, bl = split(b)
    return dot(ah, bh) + (dot(ah, bl) + dot(al, bh))


def dot3_few(a, b):
    m = a.shape[0]
    ah, al = split(a)
    bh, bl = split(b)
    both = dot(jnp.concatenate([ah, al], axis=0), bh)
    return both[:m] + (dot(ah, bl) + both[m:])


def pivot_inverse(rows):
    full = (8, NB)
    lane = lax.broadcasted_iota(jnp.int32, full, 1)
    sub = lax.broadcasted_iota(jnp.int32, full, 0)
    rows = list(rows)

    def spread(k):
        return [[jnp.broadcast_to(r[:, q : q + 1], full) for r in rows] for q in (k, k + 1)]

    c0, c1 = spread(0)
    for k in range(0, NB, 2):
        v, s = k // 8, k % 8

        def row(x, t):
            return jnp.broadcast_to(x[s + t : s + t + 1, :], full)

        r0, r1 = row(rows[v], 0), row(rows[v], 1)
        p00, p01, p10, p11 = row(c0[v], 0), row(c1[v], 0), row(c0[v], 1), row(c1[v], 1)
        scale = 1.0 / (p00 * p11 - p01 * p10)
        h00, h01, h10, h11 = p11 * scale, -(p01 * scale), -(p10 * scale), p00 * scale
        ahead = spread(k + 2) if k + 2 < NB else ()
        e0, e1 = lane == k, lane == k + 1
        r0 = jnp.where(e0, 1.0, jnp.where(e1, 0.0, r0))
        r1 = jnp.where(e1, 1.0, jnp.where(e0, 0.0, r1))
        u0 = h00 * r0 + h01 * r1
        u1 = h10 * r0 + h11 * r1
        new = []
        for d in ahead:
            b0, b1 = row(d[v], 0), row(d[v], 1)
            g0, g1 = h00 * b0 + h01 * b1, h10 * b0 + h11 * b1
            n = [d[w] - c0[w] * g0 - c1[w] * g1 for w in range(NB // 8)]
            n[v] = jnp.where(sub == s, g0, jnp.where(sub == s + 1, g1, n[v]))
            new.append(n)
        for w in range(NB // 8):
            base = jnp.where(e0 | e1, 0.0, rows[w]) - c0[w] * u0 - c1[w] * u1
            if w == v:
                base = jnp.where(sub == s, u0, jnp.where(sub == s + 1, u1, base))
            rows[w] = base
        if new:
            c0, c1 = new
    return rows


def refresh_kernel(
    scale, low_ref, tok_ref, tgt_ref, inv_ref, rows_ref, cw_ref, res_ref, cor_ref, prod_ref,
    wide_a, wide_b, row_hi, row_lo, sol_hi, sol_lo, local, every, part, heard, own_low, lows,
    s_far, r_far_up, r_far_down, s_up, s_down, r_up, r_down, own,
    z_far, zr_far_up, zr_far_down, z_up, z_down, zr_up, zr_down,
    send, recv, rs_send, rs_recv, ag_send, ag_recv,
):
    i, j, zh, x, y, zl, c = place()
    x_up, x_down = (row_of(zh, x + 1), j), (row_of(zh, x + 3), j)
    z_next, z_prev = (row_of(zh + 1, x), j), (row_of(zh + 3, x), j)
    fetch = [
        pltpu.make_async_copy(rows_ref, wide_a, local.at[0]),
        pltpu.make_async_copy(inv_ref, wide_b, local.at[1]),
        pltpu.make_async_copy(cw_ref.at[pl.ds(0, PW)], wide_a, local.at[2]),
    ]
    fetch[0].start()
    fetch[1].start()
    meet([(i, (j + d) % 16) for d in range(1, 16)] + [x_up, x_down, z_next, z_prev])
    copies = Copies(send, recv)
    tokens = tok_ref[...]
    half = low_ref.shape[0] // 2
    top, bottom = pl.ds(0, half), pl.ds(half, half)

    def rows_split():
        fetch[0].wait()
        for t in range(4):
            r = pl.ds(256 * t, 256)
            row_hi[r, :], row_lo[r, :] = split(wide_a[r, :])
        fetch[2].start()
        fetch[1].wait()

    def solve(t):
        r = pl.ds(256 * t, 256)
        bh, bl = split(wide_b[r, :])
        value = dot(bh, row_hi[...]) + (dot(bh, row_lo[...]) + dot(bl, row_hi[...]))
        sol_hi[r, :], sol_lo[r, :] = split(value)

    def remove(t):
        if t == 0:
            fetch[2].wait()
        r = pl.ds(256 * t, 256)
        ch, cl = split(wide_a[r, :])
        prod_ref[r, :] = dot(ch, sol_hi[...]) + (dot(ch, sol_lo[...]) + dot(cl, sol_hi[...]))

    partials = []

    def use(s, block):
        value = lax.dot_general(block[...], tokens, (((1,), (1,)), ((), ())), preferred_element_type=f32)
        part[s] = value
        copy = pltpu.make_async_remote_copy(
            src_ref=part.at[s],
            dst_ref=heard.at[j],
            send_sem=rs_send.at[s],
            recv_sem=rs_recv.at[j],
            device_id=(i, s),
            device_id_type=MESH,
        )
        pl.when(s != j)(copy.start)
        partials.append((s, copy))

    def spread(s, block):
        return s, copies(block, every.at[s], x_up), copies(block, every.at[s], x_down)

    zn = copies(low_ref, every.at[i], z_next)
    zp = copies(low_ref, every.at[i], z_prev)
    sent = [spread(i, low_ref)]
    use(i, low_ref)
    zn.wait_recv()
    before = row_of(zh + 3, x)
    z1 = copies(every.at[before, top], every.at[before, top], z_next)
    sent.append(spread(before, every.at[before]))
    zp.wait_recv()
    after = row_of(zh + 1, x)
    z2 = copies(every.at[after, bottom], every.at[after, bottom], z_prev)
    sent.append(spread(after, every.at[after]))
    use(before, every.at[before])
    use(after, every.at[after])
    rows_split()
    z1.wait_recv()
    z2.wait_recv()
    s = row_of(zh + 2, x)
    sent.append(spread(s, every.at[s]))
    use(s, every.at[s])
    lasts = []
    for t, (dz, (_, up, down)) in enumerate(zip((0, 3, 1, 2), sent)):
        up.wait_recv()
        before = row_of(zh + dz, x + 3)
        a = copies(every.at[before, top], every.at[before, top], x_up)
        down.wait_recv()
        after = row_of(zh + dz, x + 1)
        b = copies(every.at[after, bottom], every.at[after, bottom], x_down)
        use(before, every.at[before])
        use(after, every.at[after])
        lasts.append((dz, a, b))
        solve(t)
    for dz, a, b in lasts:
        a.wait_recv()
        b.wait_recv()
        s = row_of(zh + dz, x + 2)
        use(s, every.at[s])

    remove(0)

    total = part[j] - tgt_ref[...]
    for d in range(1, 16):
        k = (j + d) % 16
        pltpu.make_async_remote_copy(
            src_ref=part.at[k],
            dst_ref=heard.at[k],
            send_sem=rs_send.at[k],
            recv_sem=rs_recv.at[k],
            device_id=(i, k),
            device_id_type=MESH,
        ).wait_recv()
        total = total + heard[k]
    res_ref[...] = total
    own_low[...] = total.astype(bf16)

    shared = []
    for d in range(1, 16):
        copy = pltpu.make_async_remote_copy(
            src_ref=own_low,
            dst_ref=lows.at[j],
            send_sem=ag_send.at[d - 1],
            recv_sem=ag_recv.at[j],
            device_id=(i, (j + d) % 16),
            device_id_type=MESH,
        )
        copy.start()
        shared.append(copy)
    lows[j] = total.astype(bf16)
    remove(1)
    for d in range(1, 16):
        k = (j + d) % 16
        pltpu.make_async_remote_copy(
            src_ref=own_low,
            dst_ref=lows.at[k],
            send_sem=ag_send.at[d - 1],
            recv_sem=ag_recv.at[k],
            device_id=(i, k),
            device_id_type=MESH,
        ).wait_recv()

    def product(zz, xx):
        return dot(lows[row_of(zz, xx)], tokens)

    order = (2, 1, 3, 0)
    far = []
    for q, dz in enumerate(order):
        s_far[q] = product(zh + dz, x + 2).astype(bf16)
        far.append((
            copies(s_far.at[q, top], r_far_up.at[q], x_up),
            copies(s_far.at[q, bottom], r_far_down.at[q], x_down),
        ))
    remove(2)
    near = []
    for q, dz in enumerate(order):
        value = product(zh + dz, x + 1)
        far[q][0].wait_recv()
        s_up[q, top] = (value[:half] + r_far_up[q].astype(f32)).astype(bf16)
        s_up[q, bottom] = value[half:].astype(bf16)
        a = copies(s_up.at[q], r_up.at[q], x_up)
        value = product(zh + dz, x + 3)
        far[q][1].wait_recv()
        s_down[q, top] = value[:half].astype(bf16)
        s_down[q, bottom] = (value[half:] + r_far_down[q].astype(f32)).astype(bf16)
        b = copies(s_down.at[q], r_down.at[q], x_down)
        near.append((a, b))
        own[q] = product(zh + dz, x)

    remove(3)

    def joined(q):
        near[q][0].wait_recv()
        near[q][1].wait_recv()
        return own[q] + (r_up[q].astype(f32) + r_down[q].astype(f32))

    z_far[...] = joined(0).astype(bf16)
    za = copies(z_far.at[top], zr_far_up, z_next)
    zb = copies(z_far.at[bottom], zr_far_down, z_prev)
    value = joined(1)
    z_up[bottom] = value[half:].astype(bf16)
    za.wait_recv()
    z_up[top] = (value[:half] + zr_far_up[...].astype(f32)).astype(bf16)
    zc = copies(z_up, zr_up, z_next)
    value = joined(2)
    z_down[top] = value[:half].astype(bf16)
    zb.wait_recv()
    z_down[bottom] = (value[half:] + zr_far_down[...].astype(f32)).astype(bf16)
    zd = copies(z_down, zr_down, z_prev)
    value = joined(3)
    zc.wait_recv()
    zd.wait_recv()
    cor_ref[...] = (value + (zr_up[...].astype(f32) + zr_down[...].astype(f32))) * scale

    copies.drain()
    for s, copy in partials:
        pl.when(s != j)(copy.wait_send)
    for copy in shared:
        copy.wait_send()


def refresh(low, tokens, targets_t, block_inverse, rows, columns, scale):
    m, n = low.shape
    t = tokens.shape[0]
    sems = 4 + 16 + 16 + 4
    dma = pltpu.SemaphoreType.DMA

    def wide(*lead):
        return pltpu.VMEM((*lead, n), bf16)

    return pl.pallas_call(
        functools.partial(refresh_kernel, scale),
        out_shape=tuple(jax.ShapeDtypeStruct(shape, f32) for shape in ((m, t), (m, n), (n, n))),
        in_specs=[VMEM] * 3 + [pl.BlockSpec(memory_space=pl.ANY)] * 3,
        out_specs=(VMEM,) * 3,
        scratch_shapes=[
            pltpu.VMEM((n, n), f32), pltpu.VMEM((n, n), f32), wide(n), wide(n), wide(n), wide(n), dma((3,)),
            wide(16, m), pltpu.VMEM((16, m, t), f32), pltpu.VMEM((16, m, t), f32),
            pltpu.VMEM((m, t), bf16), pltpu.VMEM((16, m, t), bf16),
            wide(4, m), wide(4, m // 2), wide(4, m // 2), wide(4, m), wide(4, m), wide(4, m), wide(4, m),
            pltpu.VMEM((4, m, n), f32),
            wide(m), wide(m // 2), wide(m // 2), wide(m), wide(m), wide(m), wide(m),
            dma((sems,)), dma((sems,)), dma((16,)), dma((16,)), dma((15,)), dma((16,)),
        ],
        compiler_params=pltpu.CompilerParams(collective_id=1, has_side_effects=True, vmem_limit_bytes=52 << 20),
        cost_estimate=pl.CostEstimate(flops=10**9, bytes_accessed=200 * 10**6, transcendentals=0),
        name="refresh",
    )(low, tokens, targets_t, block_inverse, rows, columns)


def shards(panels, inverse, weight, tokens, targets):
    block_inverse, row_panel, columns, pruned, low = front(panels, inverse, weight)
    token_count = tokens.shape[0] * lax.axis_size("row")
    residual_t, correlation, update = refresh(
        low, tokens, targets.T.astype(f32), block_inverse, row_panel, columns, 1.0 / math.sqrt(token_count)
    )
    return (inverse - update, pruned, residual_t.T, correlation)


def solution(mesh):
    in_specs = (P(), P("row", "col"), P("row", "col"), P("row", "col"), P("row", "col"))
    out_specs = (P("row", "col"), P("row", "col"), P("row", "col"), P("row", "col"))
    return jax.shard_map(shards, mesh=mesh, in_specs=in_specs, out_specs=out_specs, check_vma=False)
```
